32 devices in a mesh: rep: 2 (over y), tile: 16 (over z, x, core).
Axes of the slice: x: 2, y: 2, z: 4, core: 2. Of those that a mesh axis runs over, the one named last changes fastest.
Arguments:
- inputs: bfloat16 [32, 32, 32, 320], P(('rep', 'tile')), parts along dimension 0, may hold values from -6 to 6
- out_grad: bfloat16 [32, 32, 32, 320], P(('rep', 'tile')), parts along dimension 0, may hold values from -6 to 6
- weight: bfloat16 [921600], P('tile'), may hold values from -0.109375 to 0.109375
- neighbours: int32 [16, 8], replicated, may hold values from 0 to 15, as said below
- orients: int32 [16, 8], replicated, may hold values from 0 to 3
Outputs:
- input_grad: bfloat16 [32, 32, 32, 320], P(('rep', 'tile')), parts along dimension 0
- weight_grad: float32 [1843200], P(('rep', 'tile')), parts along dimension 0
The draws below stay inside these ranges and needn't reach their ends.
There are 2 independent parts, one for each index of `rep`. The reference program is written for one: setup_inputs(seed, part) draws one part's arguments, and reference() takes and returns one part's arrays. A program takes and returns all parts, laid end to end along the dimension named above; an argument that names none is the same for every part. Nothing has to cross between parts.
Inputs may be any that keep to these rules, and one draw needn't show every extreme that they name: The tiles form 16 // 16 faces of 4 x 4 tiles, each face at 16 consecutive indices. A tile's eight neighbours are eight different tiles, none of them the tile itself.
All inputs are finite; a program needn't handle non-finite values.
Results may differ from the reference program's by a relative error of at most 0.001.
Values may be sent and summed in bfloat16 or wider, within the bound.
No kernel may reach another device: no remote copies, remote signals or barrier semaphores. Data moves between devices by JAX's collectives and lax.ppermute only.
A program may use at most 64 MiB of HBM per device.

```python
import math
import jax
import jax.numpy as jnp
from jax import lax

CH = 320
SIDE = 32
TILES = 16


def face_table(key):
    face_count = TILES // 16
    table_key = jax.random.fold_in(key, 4242)
    face_slot = jax.random.permutation(jax.random.fold_in(table_key, 1), face_count).astype(jnp.int32)
    face_turn = jax.random.randint(jax.random.fold_in(table_key, 2), (face_count,), 0, 4).astype(jnp.int32)
    slot_order = jax.random.permutation(jax.random.fold_in(table_key, 3), 16).astype(jnp.int32)
    logical = jnp.arange(TILES, dtype=jnp.int32)
    face_index = logical // 16
    tile_row = logical // 4 % 4
    tile_col = logical % 4

    def stored_index(face_ids, rows_in, cols_in):
        turn_now = face_turn[face_ids]
        placed_row = jnp.where(turn_now == 0, rows_in, jnp.where(turn_now == 1, cols_in, jnp.where(turn_now == 2, 3 - rows_in, 3 - cols_in)))
        placed_col = jnp.where(turn_now == 0, cols_in, jnp.where(turn_now == 1, 3 - rows_in, jnp.where(turn_now == 2, 3 - cols_in, rows_in)))
        return face_slot[face_ids] * 16 + slot_order[placed_row * 4 + placed_col]
    offsets = [(-1, 0), (1, 0), (0, -1), (0, 1), (-1, -1), (-1, 1), (1, -1), (1, 1)]
    neighbour_cols = []
    orient_cols = []
    for row_step, col_step in offsets:
        new_row = tile_row + row_step
        first_face = jnp.where(new_row < 0, (face_index + 1) % face_count, jnp.where(new_row > 3, (face_index + face_count - 1) % face_count, face_index))
        first_turn = jnp.where(new_row < 0, 1, jnp.where(new_row > 3, 3, 0))
        new_row = (new_row + 4) % 4
        new_col = tile_col + col_step
        second_face = jnp.where(new_col < 0, (first_face + face_count - face_count // 2) % face_count, jnp.where(new_col > 3, (first_face + face_count // 2) % face_count, first_face))
        second_turn = jnp.where(new_col < 0, 2, jnp.where(new_col > 3, 2, 0))
        new_col = (new_col + 4) % 4
        neighbour_cols.append(stored_index(second_face, new_row, new_col))
        orient_cols.append((face_turn[second_face] - face_turn[face_index] + first_turn + second_turn + 8) % 4)
    own_index = stored_index(face_index, tile_row, tile_col)
    neighbour_table = jnp.zeros((TILES, 8), jnp.int32).at[own_index].set(jnp.stack(neighbour_cols, axis=1).astype(jnp.int32))
    orient_table = jnp.zeros((TILES, 8), jnp.int32).at[own_index].set(jnp.stack(orient_cols, axis=1).astype(jnp.int32))
    return (neighbour_table, orient_table)


def draw_neighbours(key, part):
    return face_table(key)[0]


def draw_orients(key, part):
    return face_table(key)[1]


def level_of(own_key, shape, split, least, largest):
    level = 1.0
    for position, shards_of in split:
        steps = jax.random.uniform(jax.random.fold_in(jax.random.fold_in(own_key, 6), position), (shards_of,), jnp.float32, least / len(split), largest / len(split))
        level = level * jnp.repeat(jnp.exp(steps), shape[position] // shards_of).reshape((-1,) + (1,) * (len(shape) - 1 - position))
    return level


def scatter_about(stream_key, dims, width, reach, cuts=(), held_as=jnp.bfloat16):
    loudness = level_of(stream_key, dims, cuts, -0.22, 0.18) if cuts else 1.0
    drawn = jax.random.normal(stream_key, dims, jnp.float32) * width * loudness
    return jnp.minimum(jnp.maximum(drawn, -reach), reach).astype(held_as)


def setup_inputs(seed: int = 0, part: int = 0) -> dict:
    key_of = jax.random.split(jax.random.key(seed), 6)
    own_keys = jax.random.split(jax.random.fold_in(key_of[5], part), 6)
    inputs = scatter_about(own_keys[0], (TILES, SIDE, SIDE, CH), 1.0, 6.0, ((0, 16),))
    out_grad = scatter_about(own_keys[1], (TILES, SIDE, SIDE, CH), 1.0, 6.0, ((0, 16),))
    weight = scatter_about(key_of[2], (9 * CH * CH,), (9 * CH) ** -0.5, 0.109375, ((0, 16),))
    neighbours = draw_neighbours(jax.random.fold_in(key_of[5], 71), part)
    orients = draw_orients(jax.random.fold_in(key_of[5], 71), part)
    return {"inputs": inputs, "out_grad": out_grad, "weight": weight, "neighbours": neighbours, "orients": orients}


def rotate(tile, turns):
    branches = [partial_rot(k) for k in range(4)]
    return lax.switch(turns, branches, tile)

def partial_rot(count):

    def apply_rot(tile):
        return jnp.rot90(tile, count, axes=(0, 1))
    return apply_rot

def extend(out_grad, neighbours, orients, index):
    own = out_grad[index]

    def fetch(direction):
        return rotate(out_grad[neighbours[index, direction]], orients[index, direction])
    north = fetch(0)[-1, :, :]
    south = fetch(1)[0, :, :]
    west = fetch(2)[:, -1, :]
    east = fetch(3)[:, 0, :]
    north_west = fetch(4)[-1, -1, :]
    north_east = fetch(5)[-1, 0, :]
    south_west = fetch(6)[0, -1, :]
    south_east = fetch(7)[0, 0, :]
    top_row = jnp.concatenate([north_west[None], north, north_east[None]], axis=0)
    bottom_row = jnp.concatenate([south_west[None], south, south_east[None]], axis=0)
    middle = jnp.concatenate([west[:, None], own, east[:, None]], axis=1)
    return jnp.concatenate([top_row[None], middle, bottom_row[None]], axis=0)

def reference(inputs, out_grad, weight, neighbours, orients):
    kernel = weight.reshape(3, 3, CH, CH)

    def one_tile(carry, index):
        extended = extend(out_grad, neighbours, orients, index)
        flat_in = inputs[index].reshape(SIDE * SIDE, CH)
        total = jnp.zeros((SIDE * SIDE, CH), jnp.float32)
        grads = []
        for row_tap in range(3):
            for col_tap in range(3):
                window = extended[2 - row_tap:2 - row_tap + SIDE, 2 - col_tap:2 - col_tap + SIDE, :].reshape(SIDE * SIDE, CH)
                total = total + jnp.dot(window, kernel[row_tap, col_tap].T, preferred_element_type=jnp.float32)
                grads.append(jnp.dot(flat_in.T, window, preferred_element_type=jnp.float32))
        return (carry + jnp.stack(grads).reshape(3, 3, CH, CH), total.astype(jnp.bfloat16).reshape(SIDE, SIDE, CH))
    start = jnp.zeros((3, 3, CH, CH), jnp.float32)
    summed, input_grad = lax.scan(one_tile, start, jnp.arange(TILES, dtype=jnp.int32))
    scale = 1.0 / math.sqrt(TILES * SIDE * SIDE)
    return (input_grad, (summed * scale).reshape(9 * CH * CH))
```

```python
import functools
import math

import jax
import jax.numpy as jnp
from jax import lax
from jax.experimental import pallas as pl
from jax.experimental.pallas import tpu as pltpu
from jax.sharding import PartitionSpec as P

LANES = 128
GROUP = 96
VMEM = pl.BlockSpec(memory_space=pltpu.VMEM)
SMEM = pl.BlockSpec(memory_space=pltpu.SMEM)
STRIP_OF = (
    (2, 4, 1, 7),
    (0, 6, 3, 5),
    (6, 3, 5, 0),
    (4, 1, 7, 2),
    (3, 2, 0, 1),
    (2, 0, 1, 3),
    (1, 3, 2, 0),
    (0, 1, 3, 2),
)


def strip_code(direction):
    return sum(strip << (4 * turn) for turn, strip in enumerate(STRIP_OF[direction]))


def params(megabytes):
    return pltpu.CompilerParams(vmem_limit_bytes=megabytes << 20)


def pack_borders(side, count, me_ref, nbr_ref, turn_ref, grad_ref, slots_ref, strips_ref):
    pixels = side * side
    row = lax.broadcasted_iota(jnp.int32, (8 * side, 1), 0)
    strip = row // side
    step = row % side
    along = jnp.where(strip % 2 == 1, side - 1 - step, step)
    edge = strip // 2
    target = jnp.where(
        edge == 0,
        along,
        jnp.where(
            edge == 1,
            (side - 1) * side + along,
            jnp.where(edge == 2, along * side, along * side + side - 1),
        ),
    )
    column = lax.broadcasted_iota(jnp.int32, (8 * side, pixels), 1)
    pick = jnp.where(column == target, 1.0, 0.0).astype(jnp.bfloat16)
    picked = jnp.dot(pick, grad_ref[...], preferred_element_type=jnp.float32)
    strips_ref[...] = picked.astype(jnp.bfloat16).reshape(strips_ref.shape)
    me = me_ref[0]

    def fill(dest, carry):
        which = jnp.int32(0)
        for direction in range(8):
            turn = turn_ref[dest * 8 + direction]
            found = (strip_code(direction) >> (4 * turn)) & 15
            which = jnp.where(nbr_ref[dest * 8 + direction] == me, found, which)
        slots_ref[dest] = strips_ref[which]
        return carry

    lax.fori_loop(0, count, fill, 0)


def exponent_of(peak):
    return jnp.maximum(jnp.ceil(jnp.log2(jnp.maximum(peak, 1e-30))), -90.0)


def coded(block):
    power = exponent_of(jnp.max(jnp.abs(block), axis=0, keepdims=True))
    steps = jnp.round(block * (jnp.exp2(15.0 - power) * 0.999)).astype(jnp.int32)
    return steps, power.astype(jnp.int32)


def write_coded(out_ref, block, rows):
    steps, power = coded(block)
    row = lax.broadcasted_iota(jnp.int32, block.shape, 0)
    out_ref[...] = jnp.where(row == rows, power, steps).astype(jnp.int16)


def read_coded(steps, rows):
    whole = steps.astype(jnp.int32)
    power = whole[rows : rows + 1].astype(jnp.float32)
    row = lax.broadcasted_iota(jnp.int32, whole.shape, 0)
    value = whole.astype(jnp.float32) * (jnp.exp2(power - 15.0) * (1.0 / 0.999))
    return jnp.where(row == rows, 0.0, value)


def plain_weight_term(
    side, width,
    me_ref, nbr_ref, in_ref, grad_ref, slots_ref,
    left_ref, mid_ref, right_ref, acc_ref,
    in_t_ref,
):
    me = me_ref[0]
    pixels = side * side
    lanes = left_ref.shape[1]
    spare = lanes - width
    own = grad_ref[...].astype(jnp.float32)
    own = jnp.concatenate([own, jnp.zeros((pixels, spare), jnp.float32)], axis=1)
    rims = []
    for direction in range(8):
        piece = slots_ref[nbr_ref[me * 8 + direction]].astype(jnp.float32)
        rims.append(jnp.concatenate([piece, jnp.zeros((side, spare), jnp.float32)], axis=1))
    north, south, west, east = rims[:4]
    nw, ne, sw, se = [rim[0:1] for rim in rims[4:]]
    mid_ref[0:side] = north.astype(jnp.bfloat16)
    mid_ref[side : side + pixels] = own.astype(jnp.bfloat16)
    mid_ref[side + pixels :] = south.astype(jnp.bfloat16)
    place = lax.broadcasted_iota(jnp.int32, (side, side, lanes), 1)
    strip_place = lax.broadcasted_iota(jnp.int32, (side, lanes), 0)
    tall = (side, side, lanes)
    moved = pltpu.roll(own, 1, 0).reshape(tall)
    moved = jnp.where(place == 0, west.reshape(side, 1, lanes), moved)
    left_ref[side : side + pixels] = moved.reshape(pixels, lanes).astype(jnp.bfloat16)
    moved = pltpu.roll(own, pixels - 1, 0).reshape(tall)
    moved = jnp.where(place == side - 1, east.reshape(side, 1, lanes), moved)
    right_ref[side : side + pixels] = moved.reshape(pixels, lanes).astype(jnp.bfloat16)
    for start, rim, first, last in ((0, north, nw, ne), (side + pixels, south, sw, se)):
        moved = jnp.where(strip_place == 0, first, pltpu.roll(rim, 1, 0))
        left_ref[start : start + side] = moved.astype(jnp.bfloat16)
        moved = jnp.where(strip_place == side - 1, last, pltpu.roll(rim, side - 1, 0))
        right_ref[start : start + side] = moved.astype(jnp.bfloat16)
    in_t_ref[...] = in_ref[...].T
    shifted = (right_ref, mid_ref, left_ref)
    for row_tap in range(3):
        for col_tap in range(3):
            window = shifted[col_tap][(2 - row_tap) * side : (2 - row_tap) * side + pixels]
            tap = 3 * row_tap + col_tap
            term = jnp.dot(in_t_ref[...], window, preferred_element_type=jnp.float32)
            for part in range(3):
                acc_ref[part, tap * width : (tap + 1) * width] = term[
                    :, part * LANES : (part + 1) * LANES
                ]


def weight_term(
    side, width, chips, pairs,
    me_ref, nbr_ref, in_ref, grad_ref, slots_ref,
    left_ref, mid_ref, right_ref, keep_ref, send_ref,
    in_t_ref, acc_ref, pack_ref,
):
    plain_weight_term(
        side, width,
        me_ref, nbr_ref, in_ref, grad_ref, slots_ref,
        left_ref, mid_ref, right_ref, acc_ref,
        in_t_ref,
    )
    half = LANES // 2
    low = lax.broadcasted_iota(jnp.int32, (pairs, LANES), 1) < half
    for shard in range(2 * chips):
        base = shard * 2 * pairs
        even = pl.ds(base, pairs, stride=2)
        odd = pl.ds(base + 1, pairs, stride=2)
        e0, e1, e2 = [acc_ref[part, even] for part in range(3)]
        o0, o1, o2 = [pltpu.roll(acc_ref[part, odd], half, 1) for part in range(3)]
        groups = (e0, e1, jnp.where(low, e2, o0), jnp.where(low, o0, o1), jnp.where(low, o1, o2))
        for group, block in enumerate(groups):
            pack_ref[shard, group * GROUP : group * GROUP + pairs] = block
            pack_ref[shard, group * GROUP + pairs : (group + 1) * GROUP] = jnp.zeros(
                (GROUP - pairs, LANES), jnp.float32
            )
    core = me_ref[0] % 2
    for chip in range(chips):
        keep_ref[chip] = pack_ref[2 * chip + core]
        write_coded(send_ref.at[chip], pack_ref[2 * chip + 1 - core], pairs)


def pair_sum(pairs, chips, me_ref, keep_ref, got_ref, own_ref, *send_refs):
    chip = me_ref[0] // 2
    for offset in range(chips):
        dest = chip ^ offset
        total = keep_ref[dest] + read_coded(got_ref[dest], pairs)
        if offset == 0:
            own_ref[...] = total
        else:
            write_coded(send_refs[offset - 1], total, pairs)


def final_sum(pairs, scale, own_ref, *refs):
    got_refs, out_ref = refs[:-1], refs[-1]
    total = own_ref[...]
    for got_ref in got_refs:
        total = total + read_coded(got_ref[...], pairs)
    total = total * scale
    for group in range(5):
        out_ref[pl.ds(group, pairs, stride=5), :] = total[group * GROUP : group * GROUP + pairs]


def input_term(side, width, left_ref, mid_ref, right_ref, kernel_ref, out_ref):
    shifted = (right_ref, mid_ref, left_ref)
    chunk = side * side // 4
    for part in range(4):
        total = jnp.zeros((chunk, width), jnp.float32)
        for row_tap in range(3):
            for col_tap in range(3):
                start = (2 - row_tap) * side + part * chunk
                total = total + lax.dot_general(
                    shifted[col_tap][start : start + chunk, 0:width],
                    kernel_ref[3 * row_tap + col_tap],
                    (((1,), (1,)), ((), ())),
                    preferred_element_type=jnp.float32,
                )
        out_ref[part * chunk : (part + 1) * chunk] = total.astype(jnp.bfloat16)


def gather_kernel(weight, count, me):
    chips = count // 2
    piece = weight.reshape(1, -1, LANES)
    held = piece
    size = 1
    steps = []
    while size < chips:
        steps.append(size)
        size *= 2
    for step in reversed(steps):
        got = lax.ppermute(held, "tile", [(i, i ^ (2 * step)) for i in range(count)])
        held = jnp.concatenate([held, got], axis=0)
    other = lax.ppermute(held, "tile", [(i, i ^ 1) for i in range(count)])
    offsets = [0]
    for step in reversed(steps):
        offsets = offsets + [o ^ step for o in offsets]
    core = me % 2
    chip = me // 2
    first = jnp.where(core == 0, held, other)
    second = jnp.where(core == 0, other, held)
    both = jnp.stack([first, second], axis=1)
    place = jnp.asarray([offsets.index(o) for o in range(chips)], jnp.int32)
    order = place[jnp.arange(chips, dtype=jnp.int32) ^ chip]
    return both[order]


def fast_weight_grad(
    side, width, count, scale, tall, transposed, me_array, nbrs, flat_in, grad, slots
):
    chips = count // 2
    pairs = 9 * width * width // (2 * width * count)
    message = (5 * GROUP, LANES)
    left, mid, right, keep, send = pl.pallas_call(
        functools.partial(weight_term, side, width, chips, pairs),
        out_shape=(
            tall, tall, tall,
            jax.ShapeDtypeStruct((chips,) + message, jnp.float32),
            jax.ShapeDtypeStruct((chips,) + message, jnp.int16),
        ),
        in_specs=[SMEM, SMEM, VMEM, VMEM, VMEM],
        out_specs=(VMEM,) * 5,
        scratch_shapes=[
            transposed,
            pltpu.VMEM((3, 9 * width, LANES), jnp.float32),
            pltpu.VMEM((count,) + message, jnp.float32),
        ],
        compiler_params=params(56),
        name="weight_term",
    )(me_array, nbrs, flat_in, grad, slots)

    got = lax.ppermute(send, "tile", [(i, i ^ 1) for i in range(count)])
    own, *sends = pl.pallas_call(
        functools.partial(pair_sum, pairs, chips),
        out_shape=(jax.ShapeDtypeStruct(message, jnp.float32),)
        + (jax.ShapeDtypeStruct(message, jnp.int16),) * (chips - 1),
        in_specs=[SMEM, VMEM, VMEM],
        out_specs=(VMEM,) * chips,
        compiler_params=params(32),
        name="pair_sum",
    )(me_array, keep, got)
    gots = [
        lax.ppermute(sends[offset - 1], "tile", [(i, i ^ (2 * offset)) for i in range(count)])
        for offset in range(1, chips)
    ]
    weight_grad = pl.pallas_call(
        functools.partial(final_sum, pairs, scale),
        out_shape=jax.ShapeDtypeStruct((5 * pairs, LANES), jnp.float32),
        in_specs=[VMEM] * chips,
        out_specs=VMEM,
        compiler_params=params(32),
        name="final_sum",
    )(own, *gots)
    return left, mid, right, weight_grad.reshape(-1)


def per_device(inputs, out_grad, weight, neighbours, orients):
    side, width = inputs.shape[1], inputs.shape[3]
    pixels = side * side
    count = lax.axis_size("tile")
    chips = count // 2
    lanes = 3 * LANES
    me = lax.axis_index("tile")
    me_array = me.reshape(1)
    nbrs = neighbours.reshape(-1)
    turns = orients.reshape(-1)
    grad = out_grad.reshape(pixels, width)
    flat_in = inputs.reshape(pixels, width)

    slots = pl.pallas_call(
        functools.partial(pack_borders, side, count),
        out_shape=jax.ShapeDtypeStruct((count, side, width), jnp.bfloat16),
        in_specs=[SMEM, SMEM, SMEM, VMEM],
        out_specs=VMEM,
        scratch_shapes=[pltpu.VMEM((8, side, width), jnp.bfloat16)],
        compiler_params=params(32),
        name="pack_borders",
    )(me_array, nbrs, turns, grad)
    slots = lax.all_to_all(slots, "tile", 0, 0, tiled=True)

    scale = 1.0 / math.sqrt(count * inputs.shape[0] * pixels)
    tall = jax.ShapeDtypeStruct((pixels + 2 * side, lanes), jnp.bfloat16)
    transposed = pltpu.VMEM((width, pixels), jnp.bfloat16)
    if 9 * width * width % (2 * width * count):
        kernel = lax.all_gather(weight, "tile", axis=0, tiled=True).reshape(9, width, width)
        left, mid, right, parts = pl.pallas_call(
            functools.partial(plain_weight_term, side, width),
            out_shape=(tall,) * 3 + (jax.ShapeDtypeStruct((3, 9 * width, LANES), jnp.float32),),
            in_specs=[SMEM, SMEM, VMEM, VMEM, VMEM],
            out_specs=(VMEM,) * 4,
            scratch_shapes=[transposed],
            compiler_params=params(56),
            name="plain_weight_term",
        )(me_array, nbrs, flat_in, grad, slots)
        whole = jnp.concatenate(list(parts), axis=1)[:, :width].reshape(-1)
        summed = lax.psum_scatter(whole, "tile", scatter_dimension=0, tiled=True)
        weight_grad = summed * scale
    else:
        kernel = gather_kernel(weight, count, me).reshape(9, width, width)
        left, mid, right, weight_grad = fast_weight_grad(
            side, width, count, scale, tall, transposed, me_array, nbrs, flat_in, grad, slots
        )

    input_grad = pl.pallas_call(
        functools.partial(input_term, side, width),
        out_shape=jax.ShapeDtypeStruct((pixels, width), jnp.bfloat16),
        in_specs=[VMEM] * 4,
        out_specs=VMEM,
        compiler_params=params(32),
        cost_estimate=pl.CostEstimate(
            flops=18 * pixels * width * width, bytes_accessed=6 << 20, transcendentals=0
        ),
        name="input_term",
    )(left, mid, right, kernel)
    return (input_grad.reshape(inputs.shape), weight_grad)


def solution(mesh):
    in_specs = (
        P(("rep", "tile"), None, None, None),
        P(("rep", "tile"), None, None, None),
        P("tile"),
        P(),
        P(),
    )
    out_specs = (P(("rep", "tile"), None, None, None), P(("rep", "tile")))
    return jax.shard_map(
        per_device, mesh=mesh, in_specs=in_specs, out_specs=out_specs, check_vma=False
    )
```

```python
import functools
import math

import jax
import jax.numpy as jnp
from jax import lax
from jax.experimental import pallas as pl
from jax.experimental.pallas import tpu as pltpu
from jax.sharding import PartitionSpec as P

LANES = 128
GROUP = 96
VMEM = pl.BlockSpec(memory_space=pltpu.VMEM)
SMEM = pl.BlockSpec(memory_space=pltpu.SMEM)
STRIP_OF = (
    (2, 4, 1, 7),
    (0, 6, 3, 5),
    (6, 3, 5, 0),
    (4, 1, 7, 2),
    (3, 2, 0, 1),
    (2, 0, 1, 3),
    (1, 3, 2, 0),
    (0, 1, 3, 2),
)


def strip_code(direction):
    return sum(strip << (4 * turn) for turn, strip in enumerate(STRIP_OF[direction]))


def params(megabytes):
    return pltpu.CompilerParams(vmem_limit_bytes=megabytes << 20)


def low_half(rows):
    return lax.broadcasted_iota(jnp.int32, (rows, LANES), 1) < LANES // 2


def pick_pixels(rows, target, pixels, flat):
    column = lax.broadcasted_iota(jnp.int32, (rows, pixels), 1)
    pick = jnp.where(column == target, 1.0, 0.0).astype(jnp.bfloat16)
    return jnp.dot(pick, flat, preferred_element_type=jnp.float32)


def edge_pixels(side):
    row = lax.broadcasted_iota(jnp.int32, (4 * side, 1), 0)
    edge, along = row // side, row % side
    return jnp.where(
        edge == 0,
        along,
        jnp.where(
            edge == 1,
            (side - 1) * side + along,
            jnp.where(edge == 2, along * side, along * side + side - 1),
        ),
    )


def widened(block, width):
    return jnp.concatenate(
        [block, jnp.zeros((block.shape[0], 3 * LANES - width), block.dtype)], axis=1
    )


def pack_borders(side, count, me_ref, nbr_ref, turn_ref, grad_ref, slots_ref, strips_ref):
    pixels = side * side
    half = side // 2
    edges = pick_pixels(4 * side, edge_pixels(side), pixels, grad_ref[...])
    turned_row = lax.broadcasted_iota(jnp.int32, (4 * side, 4 * side), 0)
    turned_column = lax.broadcasted_iota(jnp.int32, (4 * side, 4 * side), 1)
    mirror = turned_row // side * (2 * side) + side - 1 - turned_row == turned_column
    mirror = jnp.where(mirror, 1.0, 0.0).astype(jnp.bfloat16)
    reverse = jnp.dot(mirror, edges.astype(jnp.bfloat16), preferred_element_type=jnp.float32)
    low = low_half(half)
    for flip, found in enumerate((edges, reverse)):
        found = widened(found, edges.shape[1])
        for edge in range(4):
            block = found[edge * side : (edge + 1) * side]
            last = block[:, 2 * LANES :]
            last = jnp.where(low, last[:half], pltpu.roll(last[half:], LANES // 2, 1))
            strips_ref[2 * edge + flip] = jnp.concatenate(
                [block[:, :LANES], block[:, LANES : 2 * LANES], last], axis=0
            ).astype(jnp.bfloat16)
    me = me_ref[0]

    def fill(dest, carry):
        which = jnp.int32(0)
        for direction in range(8):
            turn = turn_ref[dest, direction]
            found = (strip_code(direction) >> (4 * turn)) & 15
            which = jnp.where(nbr_ref[dest, direction] == me, found, which)
        slots_ref[dest] = strips_ref[which]
        return carry

    lax.fori_loop(0, count, fill, 0)


def rim_pieces(side, me_ref, nbr_ref, slots_ref):
    half = side // 2
    low = low_half(side)
    rims = []
    for direction in range(8):
        slot = slots_ref[nbr_ref[me_ref[0], direction]].astype(jnp.float32)
        last = slot[2 * side :]
        last = jnp.concatenate([last, pltpu.roll(last, LANES // 2, 1)], axis=0)
        last = jnp.where(low, last, 0.0)
        rims.append(jnp.concatenate([slot[:side], slot[side : 2 * side], last], axis=1))
    return rims


def row_shifts(side, rim, first, last):
    place = lax.broadcasted_iota(jnp.int32, rim.shape, 0)
    after = jnp.where(place == side - 1, last, pltpu.roll(rim, side - 1, 0))
    before = jnp.where(place == 0, first, pltpu.roll(rim, 1, 0))
    return (after, rim, before)


def fill_shifted(side, own, rims, refs):
    pixels, lanes = own.shape
    tall = (side, side, lanes)
    place = lax.broadcasted_iota(jnp.int32, tall, 1)
    after = pltpu.roll(own, pixels - 1, 0).reshape(tall)
    before = pltpu.roll(own, 1, 0).reshape(tall)
    if rims is None:
        after = jnp.where(place == side - 1, 0.0, after)
        before = jnp.where(place == 0, 0.0, before)
        outer = [[jnp.zeros((side, lanes), jnp.float32)] * 3] * 2
    else:
        north, south, west, east, nw, ne, sw, se = rims
        after = jnp.where(place == side - 1, east.reshape(side, 1, lanes), after)
        before = jnp.where(place == 0, west.reshape(side, 1, lanes), before)
        outer = [
            row_shifts(side, north, nw[0:1], ne[0:1]),
            row_shifts(side, south, sw[0:1], se[0:1]),
        ]
    for tap, block in enumerate((after.reshape(own.shape), own, before.reshape(own.shape))):
        refs[tap][0:side] = outer[0][tap].astype(jnp.bfloat16)
        refs[tap][side : side + pixels] = block.astype(jnp.bfloat16)
        refs[tap][side + pixels :] = outer[1][tap].astype(jnp.bfloat16)


def exponent_of(peak):
    return jnp.maximum(jnp.ceil(jnp.log2(jnp.maximum(peak, 1e-30))), -90.0)


def coded(block):
    power = exponent_of(jnp.max(jnp.abs(block), axis=0, keepdims=True))
    steps = jnp.round(block * (jnp.exp2(15.0 - power) * 0.999)).astype(jnp.int32)
    return steps, power.astype(jnp.int32)


def write_coded(out_ref, block, rows):
    steps, power = coded(block)
    row = lax.broadcasted_iota(jnp.int32, block.shape, 0)
    out_ref[...] = jnp.where(row == rows, power, steps).astype(jnp.int16)


def read_coded(steps, rows):
    whole = steps.astype(jnp.int32)
    power = whole[rows : rows + 1].astype(jnp.float32)
    row = lax.broadcasted_iota(jnp.int32, whole.shape, 0)
    value = whole.astype(jnp.float32) * (jnp.exp2(power - 15.0) * (1.0 / 0.999))
    return jnp.where(row == rows, 0.0, value)


def inner_term(side, width, in_ref, grad_ref, acc_ref, edge_ref, in_t_ref, *shifted):
    pixels = side * side
    own = widened(grad_ref[...].astype(jnp.float32), width)
    fill_shifted(side, own, None, shifted)
    edges = pick_pixels(4 * side, edge_pixels(side), pixels, in_ref[...])
    edge_ref[...] = edges.T.astype(jnp.bfloat16)
    in_t_ref[...] = in_ref[...].T
    for row_tap in range(3):
        for col_tap in range(3):
            window = shifted[col_tap][(2 - row_tap) * side : (2 - row_tap) * side + pixels]
            tap = 3 * row_tap + col_tap
            term = jnp.dot(in_t_ref[...], window, preferred_element_type=jnp.float32)
            for part in range(3):
                acc_ref[part, tap * width : (tap + 1) * width] = term[
                    :, part * LANES : (part + 1) * LANES
                ]


def add_rim(side, width, me_ref, nbr_ref, edge_ref, slots_ref, inner_ref, acc_ref):
    north, south, west, east, nw, ne, sw, se = rim_pieces(side, me_ref, nbr_ref, slots_ref)
    none = jnp.zeros_like(north)
    tops = row_shifts(side, north, nw[0:1], ne[0:1])
    bottoms = row_shifts(side, south, sw[0:1], se[0:1])
    lefts = row_shifts(side, west, 0.0, 0.0)
    rights = row_shifts(side, east, 0.0, 0.0)
    for row_tap in range(3):
        for col_tap in range(3):
            tap = 3 * row_tap + col_tap
            rows = slice(tap * width, (tap + 1) * width)
            if tap == 4:
                for part in range(3):
                    acc_ref[part, rows] = inner_ref[part, rows]
                continue
            outside = jnp.concatenate(
                [
                    tops[col_tap] if row_tap == 2 else none,
                    bottoms[col_tap] if row_tap == 0 else none,
                    lefts[row_tap] if col_tap == 2 else none,
                    rights[row_tap] if col_tap == 0 else none,
                ],
                axis=0,
            ).astype(jnp.bfloat16)
            term = jnp.dot(edge_ref[...], outside, preferred_element_type=jnp.float32)
            for part in range(3):
                acc_ref[part, rows] = (
                    inner_ref[part, rows] + term[:, part * LANES : (part + 1) * LANES]
                )


def rim_term(
    side, width, chips, pairs,
    me_ref, nbr_ref, edge_ref, slots_ref, inner_ref,
    keep_ref, send_ref,
    acc_ref, pack_ref,
):
    add_rim(side, width, me_ref, nbr_ref, edge_ref, slots_ref, inner_ref, acc_ref)
    half = LANES // 2
    low = low_half(pairs)
    for shard in range(2 * chips):
        base = shard * 2 * pairs
        even = pl.ds(base, pairs, stride=2)
        odd = pl.ds(base + 1, pairs, stride=2)
        e0, e1, e2 = [acc_ref[part, even] for part in range(3)]
        o0, o1, o2 = [pltpu.roll(acc_ref[part, odd], half, 1) for part in range(3)]
        groups = (e0, e1, jnp.where(low, e2, o0), jnp.where(low, o0, o1), jnp.where(low, o1, o2))
        for group, block in enumerate(groups):
            pack_ref[shard, group * GROUP : group * GROUP + pairs] = block
            pack_ref[shard, group * GROUP + pairs : (group + 1) * GROUP] = jnp.zeros(
                (GROUP - pairs, LANES), jnp.float32
            )
    core = me_ref[0] % 2
    for chip in range(chips):
        keep_ref[chip] = pack_ref[2 * chip + core]
        write_coded(send_ref.at[chip], pack_ref[2 * chip + 1 - core], pairs)


def pair_sum(pairs, chips, me_ref, keep_ref, got_ref, own_ref, *send_refs):
    chip = me_ref[0] // 2
    for offset in range(chips):
        dest = chip ^ offset
        total = keep_ref[dest] + read_coded(got_ref[dest], pairs)
        if offset == 0:
            own_ref[...] = total
        else:
            write_coded(send_refs[offset - 1], total, pairs)


def final_sum(pairs, scale, own_ref, *refs):
    got_refs, out_ref = refs[:-1], refs[-1]
    total = own_ref[...]
    for got_ref in got_refs:
        total = total + read_coded(got_ref[...], pairs)
    total = total * scale
    for group in range(5):
        out_ref[pl.ds(group, pairs, stride=5), :] = total[group * GROUP : group * GROUP + pairs]


def pack_kernel(pairs, kernel_ref, out_ref, rows_ref):
    half = LANES // 2
    low = low_half(pairs)
    rows_ref[...] = kernel_ref[...].astype(jnp.float32)
    parts = [rows_ref[pl.ds(group, pairs, stride=5), :] for group in range(5)]
    turned = [pltpu.roll(part, half, 1) for part in parts]
    groups = (
        parts[0],
        parts[1],
        jnp.where(low, turned[2], turned[3]),
        jnp.where(low, turned[3], turned[4]),
        jnp.where(low, parts[2], parts[4]),
    )
    for group, block in enumerate(groups):
        whole = jnp.concatenate([block, jnp.zeros((GROUP - pairs, LANES), jnp.float32)], axis=0)
        out_ref[0, group * GROUP : (group + 1) * GROUP] = whole.astype(jnp.bfloat16)


def unpack_kernel(pairs, places, me_ref, mine_ref, other_ref, rows_ref):
    chip = me_ref[0] // 2
    core = me_ref[0] % 2
    for offset, place in places.items():
        for source_ref, from_core in ((mine_ref, core), (other_ref, 1 - core)):
            shard = 2 * (chip ^ offset) + from_core
            base = shard * 2 * pairs
            even = pl.ds(base, pairs, stride=2)
            odd = pl.ds(base + 1, pairs, stride=2)
            e0, e1, o0, o1, last = [
                source_ref[place, group * GROUP : (group + 1) * GROUP].astype(jnp.float32)[:pairs]
                for group in range(5)
            ]
            rows_ref[0, even] = e0
            rows_ref[1, even] = e1
            rows_ref[2, even] = last
            rows_ref[0, odd] = o0
            rows_ref[1, odd] = o1
            rows_ref[2, odd] = pltpu.roll(last, LANES // 2, 1)


def input_sums(side, width, me_ref, nbr_ref, grad_ref, slots_ref, kernel_ref, out_ref, shifted):
    own = widened(grad_ref[...].astype(jnp.float32), width)
    fill_shifted(side, own, rim_pieces(side, me_ref, nbr_ref, slots_ref), shifted)
    chunk = side * side // 4
    for part in range(4):
        total = jnp.zeros((chunk, width), jnp.float32)
        for row_tap in range(3):
            for col_tap in range(3):
                start = (2 - row_tap) * side + part * chunk
                tap = 3 * row_tap + col_tap
                total = total + lax.dot_general(
                    shifted[col_tap][start : start + chunk],
                    kernel_ref[tap * width : (tap + 1) * width],
                    (((1,), (1,)), ((), ())),
                    preferred_element_type=jnp.float32,
                )
        out_ref[part * chunk : (part + 1) * chunk] = total.astype(jnp.bfloat16)


def plain_input_term(
    side, width, me_ref, nbr_ref, grad_ref, slots_ref, flat_ref, out_ref, kernel_ref, *shifted
):
    kernel_ref[...] = widened(flat_ref[...].astype(jnp.float32), width).astype(jnp.bfloat16)
    input_sums(side, width, me_ref, nbr_ref, grad_ref, slots_ref, kernel_ref, out_ref, shifted)


def input_term(
    side, width, pairs, places,
    me_ref, nbr_ref, grad_ref, slots_ref, mine_ref, other_ref,
    out_ref,
    kernel_ref, rows_ref, *shifted,
):
    unpack_kernel(pairs, places, me_ref, mine_ref, other_ref, rows_ref)
    for part in range(3):
        kernel_ref[:, part * LANES : (part + 1) * LANES] = rows_ref[part].astype(jnp.bfloat16)
    input_sums(side, width, me_ref, nbr_ref, grad_ref, slots_ref, kernel_ref, out_ref, shifted)


def after(value, *others):
    return lax.optimization_barrier((value,) + others)[0]


def gather_places(chips):
    places = [0]
    step = chips // 2
    while step:
        places = places + [offset ^ step for offset in places]
        step //= 2
    return {offset: place for place, offset in enumerate(places)}


def gather_step(held, count, step):
    got = lax.ppermute(held, "tile", [(i, i ^ (2 * step)) for i in range(count)])
    return jnp.concatenate([held, got], axis=0)


def per_device(inputs, out_grad, weight, neighbours, orients):
    side, width = inputs.shape[1], inputs.shape[3]
    pixels = side * side
    count = lax.axis_size("tile")
    chips = count // 2
    whole = 9 * width * width
    lanes = 3 * LANES
    me = lax.axis_index("tile").reshape(1)
    grad = out_grad.reshape(pixels, width)
    flat_in = inputs.reshape(pixels, width)
    scale = 1.0 / math.sqrt(count * inputs.shape[0] * pixels)
    slot = (5 * side // 2, LANES)
    shifted = [pltpu.VMEM((pixels + 2 * side, lanes), jnp.bfloat16)] * 3
    sums = (3, 9 * width, LANES)
    even = whole % (2 * width * count) == 0
    pairs = whole // (2 * width * count)
    message = (5 * GROUP, LANES)

    if even:
        packed = pl.pallas_call(
            functools.partial(pack_kernel, pairs),
            out_shape=jax.ShapeDtypeStruct((1,) + message, jnp.bfloat16),
            in_specs=[VMEM],
            out_specs=VMEM,
            scratch_shapes=[pltpu.VMEM((5 * pairs, LANES), jnp.float32)],
            name="pack_kernel",
        )(weight.reshape(-1, LANES))
        places = gather_places(chips)
        step = chips // 2
        held = gather_step(packed, count, step)
        ready_grad = after(grad, packed)
    else:
        flat_kernel = lax.all_gather(weight, "tile", axis=0, tiled=True).reshape(9 * width, width)
        ready_grad = grad

    slots = pl.pallas_call(
        functools.partial(pack_borders, side, count),
        out_shape=jax.ShapeDtypeStruct((count,) + slot, jnp.bfloat16),
        in_specs=[SMEM, SMEM, SMEM, VMEM],
        out_specs=VMEM,
        scratch_shapes=[pltpu.VMEM((8,) + slot, jnp.bfloat16)],
        compiler_params=params(32),
        name="pack_borders",
    )(me, neighbours, orients, ready_grad)
    ready_in = after(flat_in, slots)
    slots = lax.all_to_all(slots, "tile", 0, 0, tiled=True)

    inner, edges = pl.pallas_call(
        functools.partial(inner_term, side, width),
        out_shape=(
            jax.ShapeDtypeStruct(sums, jnp.float32),
            jax.ShapeDtypeStruct((width, 4 * side), jnp.bfloat16),
        ),
        in_specs=[VMEM, VMEM],
        out_specs=(VMEM, VMEM),
        scratch_shapes=[pltpu.VMEM((width, pixels), jnp.bfloat16)] + shifted,
        compiler_params=params(48),
        cost_estimate=pl.CostEstimate(
            flops=18 * pixels * width * width, bytes_accessed=6 << 20, transcendentals=0
        ),
        name="inner_term",
    )(ready_in, grad)

    if even:
        if step > 1:
            step //= 2
            held = gather_step(after(held, edges), count, step)
        keep, send = pl.pallas_call(
            functools.partial(rim_term, side, width, chips, pairs),
            out_shape=(
                jax.ShapeDtypeStruct((chips,) + message, jnp.float32),
                jax.ShapeDtypeStruct((chips,) + message, jnp.int16),
            ),
            in_specs=[SMEM, SMEM, VMEM, VMEM, VMEM],
            out_specs=(VMEM,) * 2,
            scratch_shapes=[
                pltpu.VMEM(sums, jnp.float32),
                pltpu.VMEM((count,) + message, jnp.float32),
            ],
            compiler_params=params(48),
            name="rim_term",
        )(me, neighbours, edges, slots, inner)
        while step > 1:
            step //= 2
            held = gather_step(after(held, send), count, step)
        own, gots = spread_sums(count, pairs, message, me, keep, send)
        other = lax.ppermute(after(held, own), "tile", [(i, i ^ 1) for i in range(count)])
        input_grad = pl.pallas_call(
            functools.partial(input_term, side, width, pairs, places),
            out_shape=jax.ShapeDtypeStruct((pixels, width), jnp.bfloat16),
            in_specs=[SMEM, SMEM] + [VMEM] * 4,
            out_specs=VMEM,
            scratch_shapes=[
                pltpu.VMEM((9 * width, lanes), jnp.bfloat16),
                pltpu.VMEM(sums, jnp.float32),
            ]
            + shifted,
            compiler_params=params(48),
            cost_estimate=pl.CostEstimate(
                flops=18 * pixels * width * width, bytes_accessed=6 << 20, transcendentals=0
            ),
            name="input_term",
        )(me, neighbours, grad, slots, held, other)
        weight_grad = pl.pallas_call(
            functools.partial(final_sum, pairs, scale),
            out_shape=jax.ShapeDtypeStruct((5 * pairs, LANES), jnp.float32),
            in_specs=[VMEM] * chips,
            out_specs=VMEM,
            compiler_params=params(32),
            name="final_sum",
        )(after(own, input_grad), *gots).reshape(-1)
    else:
        parts = pl.pallas_call(
            functools.partial(add_rim, side, width),
            out_shape=jax.ShapeDtypeStruct(sums, jnp.float32),
            in_specs=[SMEM, SMEM, VMEM, VMEM, VMEM],
            out_specs=VMEM,
            compiler_params=params(48),
            name="add_rim",
        )(me, neighbours, edges, slots, inner)
        flat_sums = jnp.concatenate(list(parts), axis=1)[:, :width].reshape(-1)
        weight_grad = scale * lax.psum_scatter(
            flat_sums, "tile", scatter_dimension=0, tiled=True
        )
        input_grad = pl.pallas_call(
            functools.partial(plain_input_term, side, width),
            out_shape=jax.ShapeDtypeStruct((pixels, width), jnp.bfloat16),
            in_specs=[SMEM, SMEM] + [VMEM] * 3,
            out_specs=VMEM,
            scratch_shapes=[pltpu.VMEM((9 * width, lanes), jnp.bfloat16)] + shifted,
            compiler_params=params(48),
            name="plain_input_term",
        )(me, neighbours, grad, slots, flat_kernel)
    return (input_grad.reshape(inputs.shape), weight_grad)


def spread_sums(count, pairs, message, me, keep, send):
    chips = count // 2
    got = lax.ppermute(send, "tile", [(i, i ^ 1) for i in range(count)])
    own, *sends = pl.pallas_call(
        functools.partial(pair_sum, pairs, chips),
        out_shape=(jax.ShapeDtypeStruct(message, jnp.float32),)
        + (jax.ShapeDtypeStruct(message, jnp.int16),) * (chips - 1),
        in_specs=[SMEM, VMEM, VMEM],
        out_specs=(VMEM,) * chips,
        compiler_params=params(32),
        name="pair_sum",
    )(me, keep, got)
    gots = [
        lax.ppermute(sends[offset - 1], "tile", [(i, i ^ (2 * offset)) for i in range(count)])
        for offset in range(1, chips)
    ]
    return own, gots


def solution(mesh):
    in_specs = (
        P(("rep", "tile"), None, None, None),
        P(("rep", "tile"), None, None, None),
        P("tile"),
        P(),
        P(),
    )
    out_specs = (P(("rep", "tile"), None, None, None), P(("rep", "tile")))
    return jax.shard_map(
        per_device, mesh=mesh, in_specs=in_specs, out_specs=out_specs, check_vma=False
    )
```

```python
import functools
import math

import jax
import jax.numpy as jnp
from jax import lax
from jax.experimental import pallas as pl
from jax.experimental.pallas import tpu as pltpu
from jax.sharding import PartitionSpec as P

LANES = 128
GROUP = 96
VMEM = pl.BlockSpec(memory_space=pltpu.VMEM)
SMEM = pl.BlockSpec(memory_space=pltpu.SMEM)
HBM = pl.BlockSpec(memory_space=pltpu.HBM)
STRIP_OF = (
    (2, 4, 1, 7),
    (0, 6, 3, 5),
    (6, 3, 5, 0),
    (4, 1, 7, 2),
    (3, 2, 0, 1),
    (2, 0, 1, 3),
    (1, 3, 2, 0),
    (0, 1, 3, 2),
)


def strip_code(direction):
    return sum(strip << (4 * turn) for turn, strip in enumerate(STRIP_OF[direction]))


def params(megabytes):
    return pltpu.CompilerParams(vmem_limit_bytes=megabytes << 20)


def low_half(rows):
    return lax.broadcasted_iota(jnp.int32, (rows, LANES), 1) < LANES // 2


def pick_pixels(rows, target, pixels, flat):
    column = lax.broadcasted_iota(jnp.int32, (rows, pixels), 1)
    pick = jnp.where(column == target, 1.0, 0.0).astype(jnp.bfloat16)
    return jnp.dot(pick, flat, preferred_element_type=jnp.float32)


def edge_pixels(side):
    row = lax.broadcasted_iota(jnp.int32, (4 * side, 1), 0)
    edge, along = row // side, row % side
    return jnp.where(
        edge == 0,
        along,
        jnp.where(
            edge == 1,
            (side - 1) * side + along,
            jnp.where(edge == 2, along * side, along * side + side - 1),
        ),
    )


def widened(block, width):
    return jnp.concatenate(
        [block, jnp.zeros((block.shape[0], 3 * LANES - width), block.dtype)], axis=1
    )


def pack_borders(
    side, count,
    me_ref, nbr_in_ref, turn_in_ref, grad_in_ref,
    slots_ref,
    strips_ref, top_ref, bottom_ref, left_ref, right_ref, nbr_ref, turn_ref, sems,
):
    near = left_ref.shape[1]
    half = side // 2
    copies = [
        pltpu.make_async_copy(source, held, sems.at[place])
        for place, (source, held) in enumerate(
            (
                (grad_in_ref.at[:, pl.ds(0, near)], left_ref),
                (grad_in_ref.at[:, pl.ds(side - near, near)], right_ref),
                (grad_in_ref.at[0], top_ref),
                (grad_in_ref.at[side - 1], bottom_ref),
                (nbr_in_ref, nbr_ref),
                (turn_in_ref, turn_ref),
            )
        )
    ]
    for copy in copies:
        copy.start()
    row = lax.broadcasted_iota(jnp.int32, (8 * side, 1), 0)
    edge = row // side % 4
    along = jnp.where(row < 4 * side, row % side, side - 1 - row % side)
    target = jnp.where(
        edge < 2,
        edge * side + along,
        2 * side + jnp.where(edge == 2, along * near, (side + along) * near + near - 1),
    )
    known = 2 * side + 2 * side * near
    column = lax.broadcasted_iota(jnp.int32, (8 * side, known), 1)
    pick = jnp.where(column == target, 1.0, 0.0).astype(jnp.bfloat16)
    low = low_half(half)
    for copy in copies:
        copy.wait()
    width = top_ref.shape[1]
    pixels = jnp.concatenate(
        [
            top_ref[...],
            bottom_ref[...],
            left_ref[...].reshape(side * near, width),
            right_ref[...].reshape(side * near, width),
        ],
        axis=0,
    )
    found = widened(jnp.dot(pick, pixels, preferred_element_type=jnp.float32), width)
    for strip in range(8):
        block = found[strip * side : (strip + 1) * side]
        last = block[:, 2 * LANES :]
        last = jnp.where(low, last[:half], pltpu.roll(last[half:], LANES // 2, 1))
        strips_ref[strip % 4 * 2 + strip // 4] = jnp.concatenate(
            [block[:, :LANES], block[:, LANES : 2 * LANES], last], axis=0
        ).astype(jnp.bfloat16)
    me = me_ref[0]

    def fill(dest, carry):
        which = jnp.int32(0)
        for direction in range(8):
            turn = turn_ref[direction, dest]
            found = (strip_code(direction) >> (4 * turn)) & 15
            which = jnp.where(nbr_ref[direction, dest] == me, found, which)
        slots_ref[dest] = strips_ref[which]
        return carry

    lax.fori_loop(0, count, fill, 0)


def rim_pieces(side, me_ref, nbr_ref, slots_ref):
    half = side // 2
    low = low_half(side)
    rims = []
    for direction in range(8):
        slot = slots_ref[nbr_ref[direction, me_ref[0]]].astype(jnp.float32)
        last = slot[2 * side :]
        last = jnp.concatenate([last, pltpu.roll(last, LANES // 2, 1)], axis=0)
        last = jnp.where(low, last, 0.0)
        rims.append(jnp.concatenate([slot[:side], slot[side : 2 * side], last], axis=1))
    return rims


def row_shifts(side, rim, first, last):
    place = lax.broadcasted_iota(jnp.int32, rim.shape, 0)
    after = jnp.where(place == side - 1, last, pltpu.roll(rim, side - 1, 0))
    before = jnp.where(place == 0, first, pltpu.roll(rim, 1, 0))
    return (after, rim, before)


def fill_shifted(side, own, rims, refs):
    pixels, lanes = own.shape
    tall = (side, side, lanes)
    place = lax.broadcasted_iota(jnp.int32, tall, 1)
    after = pltpu.roll(own, pixels - 1, 0).reshape(tall)
    before = pltpu.roll(own, 1, 0).reshape(tall)
    if rims is None:
        after = jnp.where(place == side - 1, 0.0, after)
        before = jnp.where(place == 0, 0.0, before)
        outer = [[jnp.zeros((side, lanes), jnp.float32)] * 3] * 2
    else:
        north, south, west, east, nw, ne, sw, se = rims
        after = jnp.where(place == side - 1, east.reshape(side, 1, lanes), after)
        before = jnp.where(place == 0, west.reshape(side, 1, lanes), before)
        outer = [
            row_shifts(side, north, nw[0:1], ne[0:1]),
            row_shifts(side, south, sw[0:1], se[0:1]),
        ]
    for tap, block in enumerate((after.reshape(own.shape), own, before.reshape(own.shape))):
        refs[tap][0:side] = outer[0][tap].astype(jnp.bfloat16)
        refs[tap][side : side + pixels] = block.astype(jnp.bfloat16)
        refs[tap][side + pixels :] = outer[1][tap].astype(jnp.bfloat16)


def exponent_of(peak):
    return jnp.maximum(jnp.ceil(jnp.log2(jnp.maximum(peak, 1e-30))), -90.0)


def coded(block):
    power = exponent_of(jnp.max(jnp.abs(block), axis=0, keepdims=True))
    steps = jnp.round(block * (jnp.exp2(15.0 - power) * 0.999)).astype(jnp.int32)
    return steps, power.astype(jnp.int32)


def write_coded(out_ref, block, rows):
    steps, power = coded(block)
    row = lax.broadcasted_iota(jnp.int32, block.shape, 0)
    out_ref[...] = jnp.where(row == rows, power, steps).astype(jnp.int16)


def read_coded(steps, rows):
    whole = steps.astype(jnp.int32)
    power = whole[rows : rows + 1].astype(jnp.float32)
    row = lax.broadcasted_iota(jnp.int32, whole.shape, 0)
    value = whole.astype(jnp.float32) * (jnp.exp2(power - 15.0) * (1.0 / 0.999))
    return jnp.where(row == rows, 0.0, value)


def inner_term(side, width, packed_ref, in_ref, grad_ref, acc_ref, edge_ref, in_t_ref, *shifted):
    pixels = side * side
    own = widened(grad_ref[...].astype(jnp.float32), width)
    fill_shifted(side, own, None, shifted)
    edges = pick_pixels(4 * side, edge_pixels(side), pixels, in_ref[...])
    edge_ref[...] = edges.T.astype(jnp.bfloat16)
    in_t_ref[...] = in_ref[...].T
    for row_tap in range(3):
        for col_tap in range(3):
            window = shifted[col_tap][(2 - row_tap) * side : (2 - row_tap) * side + pixels]
            tap = 3 * row_tap + col_tap
            term = jnp.dot(in_t_ref[...], window, preferred_element_type=jnp.float32)
            for part in range(3):
                acc_ref[part, tap * width : (tap + 1) * width] = term[
                    :, part * LANES : (part + 1) * LANES
                ]


def add_rim(side, width, me_ref, nbr_ref, edge_ref, slots_ref, inner_ref, acc_ref):
    north, south, west, east, nw, ne, sw, se = rim_pieces(side, me_ref, nbr_ref, slots_ref)
    none = jnp.zeros_like(north)
    tops = row_shifts(side, north, nw[0:1], ne[0:1])
    bottoms = row_shifts(side, south, sw[0:1], se[0:1])
    lefts = row_shifts(side, west, 0.0, 0.0)
    rights = row_shifts(side, east, 0.0, 0.0)
    for row_tap in range(3):
        for col_tap in range(3):
            tap = 3 * row_tap + col_tap
            rows = slice(tap * width, (tap + 1) * width)
            if tap == 4:
                for part in range(3):
                    acc_ref[part, rows] = inner_ref[part, rows]
                continue
            outside = jnp.concatenate(
                [
                    tops[col_tap] if row_tap == 2 else none,
                    bottoms[col_tap] if row_tap == 0 else none,
                    lefts[row_tap] if col_tap == 2 else none,
                    rights[row_tap] if col_tap == 0 else none,
                ],
                axis=0,
            ).astype(jnp.bfloat16)
            term = jnp.dot(edge_ref[...], outside, preferred_element_type=jnp.float32)
            for part in range(3):
                acc_ref[part, rows] = (
                    inner_ref[part, rows] + term[:, part * LANES : (part + 1) * LANES]
                )


def rim_term(
    side, width, chips, pairs,
    me_ref, nbr_ref, edge_ref, slots_ref, inner_ref,
    keep_ref, send_ref,
    acc_ref, pack_ref,
):
    add_rim(side, width, me_ref, nbr_ref, edge_ref, slots_ref, inner_ref, acc_ref)
    half = LANES // 2
    low = low_half(pairs)
    for shard in range(2 * chips):
        base = shard * 2 * pairs
        even = pl.ds(base, pairs, stride=2)
        odd = pl.ds(base + 1, pairs, stride=2)
        e0, e1, e2 = [acc_ref[part, even] for part in range(3)]
        o0, o1, o2 = [pltpu.roll(acc_ref[part, odd], half, 1) for part in range(3)]
        groups = (e0, e1, jnp.where(low, e2, o0), jnp.where(low, o0, o1), jnp.where(low, o1, o2))
        for group, block in enumerate(groups):
            pack_ref[shard, group * GROUP : group * GROUP + pairs] = block
            pack_ref[shard, group * GROUP + pairs : (group + 1) * GROUP] = jnp.zeros(
                (GROUP - pairs, LANES), jnp.float32
            )
    core = me_ref[0] % 2
    for chip in range(chips):
        keep_ref[chip] = pack_ref[2 * chip + core]
        write_coded(send_ref.at[chip], pack_ref[2 * chip + 1 - core], pairs)


def pair_sum(pairs, chips, me_ref, keep_ref, got_ref, own_ref, send_ref):
    across = me_ref[0] // 2 % 2
    for row in range(chips // 2):
        mine = 2 * row + across
        own_ref[row] = keep_ref[mine] + read_coded(got_ref[mine], pairs)
        theirs = 2 * row + 1 - across
        write_coded(
            send_ref.at[row], keep_ref[theirs] + read_coded(got_ref[theirs], pairs), pairs
        )


def cross_sum(pairs, rows, me_ref, keep_ref, got_ref, own_ref, *send_refs):
    for offset in range(rows):
        row = (me_ref[0] // 4) ^ offset
        total = keep_ref[row] + read_coded(got_ref[row], pairs)
        if offset == 0:
            own_ref[...] = total
        else:
            write_coded(send_refs[offset - 1], total, pairs)


def final_sum(pairs, scale, own_ref, *refs):
    got_refs, out_ref = refs[:-1], refs[-1]
    total = own_ref[...]
    for got_ref in got_refs:
        total = total + read_coded(got_ref[...], pairs)
    total = total * scale
    for group in range(5):
        out_ref[pl.ds(group, pairs, stride=5), :] = total[group * GROUP : group * GROUP + pairs]


def unpack_kernel(pairs, chips, me_ref, mine_ref, other_ref, shard_ref, rows_ref):
    chip = me_ref[0] // 2
    core = me_ref[0] % 2
    half = LANES // 2
    low = low_half(pairs)
    turn = 0
    for offset in range(chips):
        for source_ref, from_core in ((mine_ref, core), (other_ref, 1 - core)):
            shard = 2 * (chip ^ offset) + from_core
            base = shard * 2 * pairs
            even = pl.ds(base, pairs, stride=2)
            odd = pl.ds(base + 1, pairs, stride=2)
            shard_ref[turn] = source_ref[offset].astype(jnp.float32)[: 5 * pairs]
            parts = [shard_ref[turn, pl.ds(group, pairs, stride=5), :] for group in range(5)]
            turned = [pltpu.roll(part, half, 1) for part in parts[2:]]
            rows_ref[0, even] = parts[0]
            rows_ref[1, even] = parts[1]
            rows_ref[2, even] = parts[2]
            rows_ref[0, odd] = jnp.where(low, turned[0], turned[1])
            rows_ref[1, odd] = jnp.where(low, turned[1], turned[2])
            rows_ref[2, odd] = turned[2]
            turn = 1 - turn


def input_sums(side, width, me_ref, nbr_ref, grad_ref, slots_ref, kernel_ref, out_ref, shifted):
    own = widened(grad_ref[...].astype(jnp.float32), width)
    fill_shifted(side, own, rim_pieces(side, me_ref, nbr_ref, slots_ref), shifted)
    chunk = side * side // 4
    for part in range(4):
        total = jnp.zeros((chunk, width), jnp.float32)
        for row_tap in range(3):
            for col_tap in range(3):
                start = (2 - row_tap) * side + part * chunk
                tap = 3 * row_tap + col_tap
                total = total + lax.dot_general(
                    shifted[col_tap][start : start + chunk],
                    kernel_ref[tap * width : (tap + 1) * width],
                    (((1,), (1,)), ((), ())),
                    preferred_element_type=jnp.float32,
                )
        out_ref[part * chunk : (part + 1) * chunk] = total.astype(jnp.bfloat16)


def plain_input_term(
    side, width, me_ref, nbr_ref, grad_ref, slots_ref, flat_ref, out_ref, kernel_ref, *shifted
):
    kernel_ref[...] = widened(flat_ref[...].astype(jnp.float32), width).astype(jnp.bfloat16)
    input_sums(side, width, me_ref, nbr_ref, grad_ref, slots_ref, kernel_ref, out_ref, shifted)


def input_term(
    side, width, pairs, chips,
    me_ref, nbr_ref, grad_ref, slots_ref, mine_ref, other_ref,
    out_ref,
    kernel_ref, shard_ref, rows_ref, *shifted,
):
    unpack_kernel(pairs, chips, me_ref, mine_ref, other_ref, shard_ref, rows_ref)
    for part in range(3):
        kernel_ref[:, part * LANES : (part + 1) * LANES] = rows_ref[part].astype(jnp.bfloat16)
    input_sums(side, width, me_ref, nbr_ref, grad_ref, slots_ref, kernel_ref, out_ref, shifted)


def after(value, *others):
    return lax.optimization_barrier((value,) + others)[0]


def from_offset(value, count, offset):
    return lax.ppermute(value, "tile", [(i, i ^ (2 * offset)) for i in range(count)])


def per_device(inputs, out_grad, weight, neighbours, orients):
    side, width = inputs.shape[1], inputs.shape[3]
    pixels = side * side
    count = lax.axis_size("tile")
    chips = count // 2
    whole = 9 * width * width
    lanes = 3 * LANES
    me = lax.axis_index("tile").reshape(1)
    neighbours, orients = neighbours.T, orients.T
    grad = out_grad.reshape(pixels, width)
    flat_in = inputs.reshape(pixels, width)
    scale = 1.0 / math.sqrt(count * inputs.shape[0] * pixels)
    slot = (5 * side // 2, LANES)
    shifted = [pltpu.VMEM((pixels + 2 * side, lanes), jnp.bfloat16)] * 3
    sums = (3, 9 * width, LANES)
    even = count == 16 and whole % (2 * width * count) == 0
    pairs = whole // (2 * width * count)
    message = (5 * GROUP, LANES)

    if not even:
        flat_kernel = lax.all_gather(weight, "tile", axis=0, tiled=True).reshape(9 * width, width)

    slots = pl.pallas_call(
        functools.partial(pack_borders, side, count),
        out_shape=jax.ShapeDtypeStruct((count,) + slot, jnp.bfloat16),
        in_specs=[SMEM, HBM, HBM, HBM],
        out_specs=VMEM,
        scratch_shapes=[
            pltpu.VMEM((8,) + slot, jnp.bfloat16),
            pltpu.VMEM((side, width), jnp.bfloat16),
            pltpu.VMEM((side, width), jnp.bfloat16),
            pltpu.VMEM((side, 8, width), jnp.bfloat16),
            pltpu.VMEM((side, 8, width), jnp.bfloat16),
            pltpu.SMEM(neighbours.shape, jnp.int32),
            pltpu.SMEM(orients.shape, jnp.int32),
            pltpu.SemaphoreType.DMA((6,)),
        ],
        compiler_params=params(60),
        name="pack_borders",
    )(me, neighbours, orients, out_grad[0])
    packed = after(me, slots)
    if even:
        shard = after(weight, slots).reshape(1, -1, LANES)
        shard = jnp.pad(shard, ((0, 0), (0, -shard.shape[1] % 16), (0, 0)))
        held = jnp.concatenate([shard, from_offset(shard, count, 1)], axis=0)
    slots = lax.all_to_all(slots, "tile", 0, 0, tiled=True)

    inner, edges = pl.pallas_call(
        functools.partial(inner_term, side, width),
        out_shape=(
            jax.ShapeDtypeStruct(sums, jnp.float32),
            jax.ShapeDtypeStruct((width, 4 * side), jnp.bfloat16),
        ),
        in_specs=[SMEM, VMEM, VMEM],
        out_specs=(VMEM, VMEM),
        scratch_shapes=[pltpu.VMEM((width, pixels), jnp.bfloat16)] + shifted,
        compiler_params=params(20),
        cost_estimate=pl.CostEstimate(
            flops=18 * pixels * width * width, bytes_accessed=6 << 20, transcendentals=0
        ),
        name="inner_term",
    )(packed, flat_in, grad)

    if even:
        keep, send = pl.pallas_call(
            functools.partial(rim_term, side, width, chips, pairs),
            out_shape=(
                jax.ShapeDtypeStruct((chips,) + message, jnp.float32),
                jax.ShapeDtypeStruct((chips,) + message, jnp.int16),
            ),
            in_specs=[SMEM, SMEM, VMEM, VMEM, VMEM],
            out_specs=(VMEM,) * 2,
            scratch_shapes=[
                pltpu.VMEM(sums, jnp.float32),
                pltpu.VMEM((count,) + message, jnp.float32),
            ],
            compiler_params=params(20),
            name="rim_term",
        )(after(me, held), neighbours, edges, slots, inner)
        second = from_offset(held, count, 2)
        third = from_offset(held, count, 4)
        own, got, crossing = spread_sums(count, pairs, message, me, keep, send)
        third = after(third, crossing, second)
        last = after(from_offset(third, count, 2), own, got[2])
        held = jnp.concatenate([held, second, third, last], axis=0)
        other = lax.ppermute(after(held, own), "tile", [(i, i ^ 1) for i in range(count)])
        input_grad = pl.pallas_call(
            functools.partial(input_term, side, width, pairs, chips),
            out_shape=jax.ShapeDtypeStruct((pixels, width), jnp.bfloat16),
            in_specs=[SMEM, SMEM] + [VMEM] * 4,
            out_specs=VMEM,
            scratch_shapes=[
                pltpu.VMEM((9 * width, lanes), jnp.bfloat16),
                pltpu.VMEM((2, 5 * pairs, LANES), jnp.float32),
                pltpu.VMEM(sums, jnp.float32),
            ]
            + shifted,
            compiler_params=params(26),
            cost_estimate=pl.CostEstimate(
                flops=18 * pixels * width * width, bytes_accessed=6 << 20, transcendentals=0
            ),
            name="input_term",
        )(me, neighbours, grad, slots, held, other)
        weight_grad = pl.pallas_call(
            functools.partial(final_sum, pairs, scale),
            out_shape=jax.ShapeDtypeStruct((5 * pairs, LANES), jnp.float32),
            in_specs=[VMEM] * (count // 4),
            out_specs=VMEM,
            compiler_params=params(8),
            name="final_sum",
        )(after(own, input_grad), *got).reshape(-1)
    else:
        parts = pl.pallas_call(
            functools.partial(add_rim, side, width),
            out_shape=jax.ShapeDtypeStruct(sums, jnp.float32),
            in_specs=[SMEM, SMEM, VMEM, VMEM, VMEM],
            out_specs=VMEM,
            compiler_params=params(20),
            name="add_rim",
        )(me, neighbours, edges, slots, inner)
        flat_sums = jnp.concatenate(list(parts), axis=1)[:, :width].reshape(-1)
        weight_grad = scale * lax.psum_scatter(
            flat_sums, "tile", scatter_dimension=0, tiled=True
        )
        input_grad = pl.pallas_call(
            functools.partial(plain_input_term, side, width),
            out_shape=jax.ShapeDtypeStruct((pixels, width), jnp.bfloat16),
            in_specs=[SMEM, SMEM] + [VMEM] * 3,
            out_specs=VMEM,
            scratch_shapes=[pltpu.VMEM((9 * width, lanes), jnp.bfloat16)] + shifted,
            compiler_params=params(26),
            name="plain_input_term",
        )(me, neighbours, grad, slots, flat_kernel)
    return (input_grad.reshape(inputs.shape), weight_grad)


def spread_sums(count, pairs, message, me, keep, send):
    rows = count // 4
    several = jax.ShapeDtypeStruct((rows,) + message, jnp.float32)
    coded_several = jax.ShapeDtypeStruct((rows,) + message, jnp.int16)
    got = lax.ppermute(send, "tile", [(i, i ^ 1) for i in range(count)])
    keep, send = pl.pallas_call(
        functools.partial(pair_sum, pairs, count // 2),
        out_shape=(several, coded_several),
        in_specs=[SMEM, VMEM, VMEM],
        out_specs=(VMEM,) * 2,
        compiler_params=params(12),
        name="pair_sum",
    )(me, keep, got)
    crossing = send
    got = from_offset(send, count, 1)
    own, *sends = pl.pallas_call(
        functools.partial(cross_sum, pairs, rows),
        out_shape=(jax.ShapeDtypeStruct(message, jnp.float32),)
        + (jax.ShapeDtypeStruct(message, jnp.int16),) * (rows - 1),
        in_specs=[SMEM, VMEM, VMEM],
        out_specs=(VMEM,) * rows,
        compiler_params=params(12),
        name="cross_sum",
    )(me, keep, got)
    got = [from_offset(sends[offset - 1], count, 2 * offset) for offset in range(1, rows)]
    return own, got, crossing


def solution(mesh):
    in_specs = (
        P(("rep", "tile"), None, None, None),
        P(("rep", "tile"), None, None, None),
        P("tile"),
        P(),
        P(),
    )
    out_specs = (P(("rep", "tile"), None, None, None), P(("rep", "tile")))
    return jax.shard_map(
        per_device, mesh=mesh, in_specs=in_specs, out_specs=out_specs, check_vma=False
    )
```

```python
import functools
import math

import jax
import jax.numpy as jnp
from jax import lax
from jax.experimental import pallas as pl
from jax.experimental.pallas import tpu as pltpu
from jax.sharding import PartitionSpec as P

LANES = 128
GROUP = 96
VMEM = pl.BlockSpec(memory_space=pltpu.VMEM)
SMEM = pl.BlockSpec(memory_space=pltpu.SMEM)
HBM = pl.BlockSpec(memory_space=pltpu.HBM)
STRIP_OF = (
    (2, 4, 1, 7),
    (0, 6, 3, 5),
    (6, 3, 5, 0),
    (4, 1, 7, 2),
    (3, 2, 0, 1),
    (2, 0, 1, 3),
    (1, 3, 2, 0),
    (0, 1, 3, 2),
)


def strip_code(direction):
    return sum(strip << (4 * turn) for turn, strip in enumerate(STRIP_OF[direction]))


def params(megabytes):
    return pltpu.CompilerParams(vmem_limit_bytes=megabytes << 20)


def low_half(rows):
    return lax.broadcasted_iota(jnp.int32, (rows, LANES), 1) < LANES // 2


def pick_pixels(rows, target, pixels, flat):
    column = lax.broadcasted_iota(jnp.int32, (rows, pixels), 1)
    pick = jnp.where(column == target, 1.0, 0.0).astype(jnp.bfloat16)
    return jnp.dot(pick, flat, preferred_element_type=jnp.float32)


def edge_pixels(side):
    row = lax.broadcasted_iota(jnp.int32, (4 * side, 1), 0)
    edge, along = row // side, row % side
    return jnp.where(
        edge == 0,
        along,
        jnp.where(
            edge == 1,
            (side - 1) * side + along,
            jnp.where(edge == 2, along * side, along * side + side - 1),
        ),
    )


def widened(block, width):
    return jnp.concatenate(
        [block, jnp.zeros((block.shape[0], 3 * LANES - width), block.dtype)], axis=1
    )


def pack_borders(
    side, count,
    me_ref, nbr_in_ref, turn_in_ref, grad_in_ref,
    slots_ref,
    strips_ref, top_ref, bottom_ref, left_ref, right_ref, nbr_ref, turn_ref, which_ref, sems,
):
    near = left_ref.shape[1]
    half = side // 2
    copies = [
        pltpu.make_async_copy(source, held, sems.at[place])
        for place, (source, held) in enumerate(
            (
                (grad_in_ref.at[:, pl.ds(0, near)], left_ref),
                (grad_in_ref.at[:, pl.ds(side - near, near)], right_ref),
                (grad_in_ref.at[0], top_ref),
                (grad_in_ref.at[side - 1], bottom_ref),
                (nbr_in_ref, nbr_ref),
                (turn_in_ref, turn_ref),
            )
        )
    ]
    for copy in copies:
        copy.start()
    row = lax.broadcasted_iota(jnp.int32, (8 * side, 1), 0)
    edge = row // side % 4
    along = jnp.where(row < 4 * side, row % side, side - 1 - row % side)
    target = jnp.where(
        edge < 2,
        edge * side + along,
        2 * side + jnp.where(edge == 2, along * near, (side + along) * near + near - 1),
    )
    known = 2 * side + 2 * side * near
    column = lax.broadcasted_iota(jnp.int32, (8 * side, known), 1)
    pick = jnp.where(column == target, 1.0, 0.0).astype(jnp.bfloat16)
    low = low_half(half)
    me = me_ref[0]
    for copy in copies[4:]:
        copy.wait()

    def choose(dest, carry):
        which = jnp.int32(0)
        for direction in range(8):
            turn = turn_ref[direction, dest]
            found = (strip_code(direction) >> (4 * turn)) & 15
            which = jnp.where(nbr_ref[direction, dest] == me, found, which)
        which_ref[dest] = which
        return carry

    lax.fori_loop(0, count, choose, 0, unroll=4)
    for copy in copies[:4]:
        copy.wait()
    width = top_ref.shape[1]
    pixels = jnp.concatenate(
        [
            top_ref[...],
            bottom_ref[...],
            left_ref[...].reshape(side * near, width),
            right_ref[...].reshape(side * near, width),
        ],
        axis=0,
    )
    found = widened(jnp.dot(pick, pixels, preferred_element_type=jnp.float32), width)
    for strip in range(8):
        block = found[strip * side : (strip + 1) * side]
        last = block[:, 2 * LANES :]
        last = jnp.where(low, last[:half], pltpu.roll(last[half:], LANES // 2, 1))
        strips_ref[strip % 4 * 2 + strip // 4] = jnp.concatenate(
            [block[:, :LANES], block[:, LANES : 2 * LANES], last], axis=0
        ).astype(jnp.bfloat16)

    def fill(dest, carry):
        slots_ref[dest] = strips_ref[which_ref[dest]]
        return carry

    lax.fori_loop(0, count, fill, 0, unroll=8)


def rim_pieces(side, me_ref, nbr_ref, slots_ref):
    half = side // 2
    low = low_half(side)
    rims = []
    for direction in range(8):
        slot = slots_ref[nbr_ref[direction, me_ref[0]]].astype(jnp.float32)
        last = slot[2 * side :]
        last = jnp.concatenate([last, pltpu.roll(last, LANES // 2, 1)], axis=0)
        last = jnp.where(low, last, 0.0)
        rims.append(jnp.concatenate([slot[:side], slot[side : 2 * side], last], axis=1))
    return rims


def row_shifts(side, rim, first, last):
    place = lax.broadcasted_iota(jnp.int32, rim.shape, 0)
    after = jnp.where(place == side - 1, last, pltpu.roll(rim, side - 1, 0))
    before = jnp.where(place == 0, first, pltpu.roll(rim, 1, 0))
    return (after, rim, before)


def fill_shifted(side, own, rims, ref):
    pixels, lanes = own.shape
    tall = (side, side, lanes)
    place = lax.broadcasted_iota(jnp.int32, tall, 1)
    after = pltpu.roll(own, pixels - 1, 0).reshape(tall)
    before = pltpu.roll(own, 1, 0).reshape(tall)
    if rims is None:
        after = jnp.where(place == side - 1, 0.0, after)
        before = jnp.where(place == 0, 0.0, before)
        outer = [[jnp.zeros((side, lanes), jnp.float32)] * 3] * 2
    else:
        north, south, west, east, nw, ne, sw, se = rims
        after = jnp.where(place == side - 1, east.reshape(side, 1, lanes), after)
        before = jnp.where(place == 0, west.reshape(side, 1, lanes), before)
        outer = [
            row_shifts(side, north, nw[0:1], ne[0:1]),
            row_shifts(side, south, sw[0:1], se[0:1]),
        ]
    for tap, block in enumerate((after.reshape(own.shape), own, before.reshape(own.shape))):
        place = slice(tap * lanes, (tap + 1) * lanes)
        ref[0:side, place] = outer[0][tap].astype(jnp.bfloat16)
        ref[side : side + pixels, place] = block.astype(jnp.bfloat16)
        ref[side + pixels :, place] = outer[1][tap].astype(jnp.bfloat16)


def exponent_of(peak):
    return jnp.maximum(jnp.ceil(jnp.log2(jnp.maximum(peak, 1e-30))), -90.0)


def coded(block):
    power = exponent_of(jnp.max(jnp.abs(block), axis=0, keepdims=True))
    steps = jnp.round(block * (jnp.exp2(15.0 - power) * 0.999)).astype(jnp.int32)
    return steps, power.astype(jnp.int32)


def write_coded(out_ref, block, rows):
    steps, power = coded(block)
    row = lax.broadcasted_iota(jnp.int32, block.shape, 0)
    out_ref[...] = jnp.where(row == rows, power, steps).astype(jnp.int16)


def read_coded(steps, rows):
    whole = steps.astype(jnp.int32)
    power = whole[rows : rows + 1].astype(jnp.float32)
    row = lax.broadcasted_iota(jnp.int32, whole.shape, 0)
    value = whole.astype(jnp.float32) * (jnp.exp2(power - 15.0) * (1.0 / 0.999))
    return jnp.where(row == rows, 0.0, value)


def inner_term(side, width, packed_ref, in_ref, grad_ref, acc_ref, edge_ref, in_t_ref, shifted):
    pixels = side * side
    own = widened(grad_ref[...].astype(jnp.float32), width)
    fill_shifted(side, own, None, shifted)
    edges = pick_pixels(4 * side, edge_pixels(side), pixels, in_ref[...])
    edge_ref[...] = edges.T.astype(jnp.bfloat16)
    in_t_ref[...] = in_ref[...].T
    for row_tap in range(3):
        window = shifted[(2 - row_tap) * side : (2 - row_tap) * side + pixels]
        term = jnp.dot(in_t_ref[...], window, preferred_element_type=jnp.float32)
        for col_tap in range(3):
            tap = 3 * row_tap + col_tap
            for part in range(3):
                place = (3 * col_tap + part) * LANES
                acc_ref[part, tap * width : (tap + 1) * width] = term[:, place : place + LANES]


def add_rim(side, width, me_ref, nbr_ref, edge_ref, slots_ref, inner_ref, acc_ref):
    north, south, west, east, nw, ne, sw, se = rim_pieces(side, me_ref, nbr_ref, slots_ref)
    none = jnp.zeros_like(north)
    tops = row_shifts(side, north, nw[0:1], ne[0:1])
    bottoms = row_shifts(side, south, sw[0:1], se[0:1])
    lefts = row_shifts(side, west, 0.0, 0.0)
    rights = row_shifts(side, east, 0.0, 0.0)
    for row_tap in range(3):
        for col_tap in range(3):
            tap = 3 * row_tap + col_tap
            rows = slice(tap * width, (tap + 1) * width)
            if tap == 4:
                for part in range(3):
                    acc_ref[part, rows] = inner_ref[part, rows]
                continue
            outside = jnp.concatenate(
                [
                    tops[col_tap] if row_tap == 2 else none,
                    bottoms[col_tap] if row_tap == 0 else none,
                    lefts[row_tap] if col_tap == 2 else none,
                    rights[row_tap] if col_tap == 0 else none,
                ],
                axis=0,
            ).astype(jnp.bfloat16)
            term = jnp.dot(edge_ref[...], outside, preferred_element_type=jnp.float32)
            for part in range(3):
                acc_ref[part, rows] = (
                    inner_ref[part, rows] + term[:, part * LANES : (part + 1) * LANES]
                )


def rim_term(
    side, width, chips, pairs,
    me_ref, nbr_ref, edge_ref, slots_ref, inner_ref,
    keep_ref, send_ref,
    acc_ref, pack_ref,
):
    add_rim(side, width, me_ref, nbr_ref, edge_ref, slots_ref, inner_ref, acc_ref)
    half = LANES // 2
    low = low_half(pairs)
    core = me_ref[0] % 2
    blank = jnp.zeros((GROUP - pairs, LANES), jnp.float32)
    for chip in range(chips):
        for shard, out_ref in (
            (2 * chip + core, keep_ref.at[chip]),
            (2 * chip + 1 - core, pack_ref.at[chip % 2]),
        ):
            base = shard * 2 * pairs
            even = pl.ds(base, pairs, stride=2)
            odd = pl.ds(base + 1, pairs, stride=2)
            e0, e1, e2 = [acc_ref[part, even] for part in range(3)]
            o0, o1, o2 = [pltpu.roll(acc_ref[part, odd], half, 1) for part in range(3)]
            groups = (
                e0,
                e1,
                jnp.where(low, e2, o0),
                jnp.where(low, o0, o1),
                jnp.where(low, o1, o2),
            )
            for group, block in enumerate(groups):
                out_ref[group * GROUP : group * GROUP + pairs] = block
                out_ref[group * GROUP + pairs : (group + 1) * GROUP] = blank
        write_coded(send_ref.at[chip], pack_ref[chip % 2], pairs)


def pair_sum(pairs, chips, me_ref, keep_ref, got_ref, own_ref, send_ref):
    across = me_ref[0] // 2 % 2
    for row in range(chips // 2):
        mine = 2 * row + across
        own_ref[row] = keep_ref[mine] + read_coded(got_ref[mine], pairs)
        theirs = 2 * row + 1 - across
        write_coded(
            send_ref.at[row], keep_ref[theirs] + read_coded(got_ref[theirs], pairs), pairs
        )


def cross_sum(pairs, rows, me_ref, keep_ref, got_ref, own_ref, *send_refs):
    for offset in range(rows):
        row = (me_ref[0] // 4) ^ offset
        total = keep_ref[row] + read_coded(got_ref[row], pairs)
        if offset == 0:
            own_ref[...] = total
        else:
            write_coded(send_refs[offset - 1], total, pairs)


def final_sum(pairs, scale, own_ref, *refs):
    got_refs, out_ref = refs[:-1], refs[-1]
    total = own_ref[...]
    for got_ref in got_refs:
        total = total + read_coded(got_ref[...], pairs)
    total = total * scale
    for group in range(5):
        out_ref[pl.ds(group, pairs, stride=5), :] = total[group * GROUP : group * GROUP + pairs]


def unpack_kernel(pairs, chips, me_ref, mine_ref, other_ref, shard_ref, rows_ref):
    chip = me_ref[0] // 2
    core = me_ref[0] % 2
    half = LANES // 2
    low = low_half(pairs)
    turn = 0
    for offset in range(chips):
        for source_ref, from_core in ((mine_ref, core), (other_ref, 1 - core)):
            shard = 2 * (chip ^ offset) + from_core
            base = shard * 2 * pairs
            even = pl.ds(base, pairs, stride=2)
            odd = pl.ds(base + 1, pairs, stride=2)
            shard_ref[turn] = source_ref[offset].astype(jnp.float32)[: 5 * pairs]
            parts = [shard_ref[turn, pl.ds(group, pairs, stride=5), :] for group in range(5)]
            turned = [pltpu.roll(part, half, 1) for part in parts[2:]]
            rows_ref[0, even] = parts[0]
            rows_ref[1, even] = parts[1]
            rows_ref[2, even] = parts[2]
            rows_ref[0, odd] = jnp.where(low, turned[0], turned[1])
            rows_ref[1, odd] = jnp.where(low, turned[1], turned[2])
            rows_ref[2, odd] = turned[2]
            turn = 1 - turn


def input_sums(side, width, me_ref, nbr_ref, grad_ref, slots_ref, kernel_ref, out_ref, shifted):
    own = widened(grad_ref[...].astype(jnp.float32), width)
    fill_shifted(side, own, rim_pieces(side, me_ref, nbr_ref, slots_ref), shifted)
    pixels = side * side
    main = 2 * LANES
    rest = width - main
    total = jnp.zeros((pixels, main), jnp.float32)
    for row_tap in range(3):
        total = total + lax.dot_general(
            shifted[(2 - row_tap) * side : (2 - row_tap) * side + pixels],
            kernel_ref[row_tap * width : row_tap * width + main],
            (((1,), (1,)), ((), ())),
            preferred_element_type=jnp.float32,
        )
    out_ref[:, :main] = total.astype(jnp.bfloat16)
    tails = lax.dot_general(
        shifted[...],
        jnp.concatenate(
            [kernel_ref[tap * width + main : (tap + 1) * width] for tap in range(3)], axis=0
        ),
        (((1,), (1,)), ((), ())),
        preferred_element_type=jnp.float32,
    )
    first = tails[2 * side : 2 * side + pixels, :rest]
    second = tails[side : side + pixels, rest : 2 * rest]
    third = tails[:pixels, 2 * rest :]
    out_ref[:, main:] = (first + second + third).astype(jnp.bfloat16)


def plain_input_term(
    side, width, me_ref, nbr_ref, grad_ref, slots_ref, flat_ref, out_ref, kernel_ref, shifted
):
    for tap in range(9):
        rows = widened(flat_ref[tap * width : (tap + 1) * width].astype(jnp.float32), width)
        place = tap % 3 * rows.shape[1]
        kernel_ref[
            tap // 3 * width : (tap // 3 + 1) * width, place : place + rows.shape[1]
        ] = rows.astype(jnp.bfloat16)
    input_sums(side, width, me_ref, nbr_ref, grad_ref, slots_ref, kernel_ref, out_ref, shifted)


def input_term(
    side, width, pairs, chips,
    me_ref, nbr_ref, grad_ref, slots_ref, mine_ref, other_ref,
    out_ref,
    kernel_ref, shard_ref, rows_ref, shifted,
):
    unpack_kernel(pairs, chips, me_ref, mine_ref, other_ref, shard_ref, rows_ref)
    for tap in range(9):
        for part in range(3):
            place = (tap % 3 * 3 + part) * LANES
            kernel_ref[
                tap // 3 * width : (tap // 3 + 1) * width, place : place + LANES
            ] = rows_ref[part, tap * width : (tap + 1) * width].astype(jnp.bfloat16)
    input_sums(side, width, me_ref, nbr_ref, grad_ref, slots_ref, kernel_ref, out_ref, shifted)


def after(value, *others):
    return lax.optimization_barrier((value,) + others)[0]


def from_offset(value, count, offset):
    return lax.ppermute(value, "tile", [(i, i ^ (2 * offset)) for i in range(count)])


def per_device(inputs, out_grad, weight, neighbours, orients):
    side, width = inputs.shape[1], inputs.shape[3]
    pixels = side * side
    count = lax.axis_size("tile")
    chips = count // 2
    whole = 9 * width * width
    lanes = 3 * LANES
    me = lax.axis_index("tile").reshape(1)
    neighbours, orients = neighbours.T, orients.T
    grad = out_grad.reshape(pixels, width)
    flat_in = inputs.reshape(pixels, width)
    scale = 1.0 / math.sqrt(count * inputs.shape[0] * pixels)
    slot = (5 * side // 2, LANES)
    shifted = [pltpu.VMEM((pixels + 2 * side, 3 * lanes), jnp.bfloat16)]
    sums = (3, 9 * width, LANES)
    even = count == 16 and whole % (2 * width * count) == 0
    pairs = whole // (2 * width * count)
    message = (5 * GROUP, LANES)

    if not even:
        flat_kernel = lax.all_gather(weight, "tile", axis=0, tiled=True).reshape(9 * width, width)

    slots = pl.pallas_call(
        functools.partial(pack_borders, side, count),
        out_shape=jax.ShapeDtypeStruct((count,) + slot, jnp.bfloat16),
        in_specs=[SMEM, HBM, HBM, HBM],
        out_specs=VMEM,
        scratch_shapes=[
            pltpu.VMEM((8,) + slot, jnp.bfloat16),
            pltpu.VMEM((side, width), jnp.bfloat16),
            pltpu.VMEM((side, width), jnp.bfloat16),
            pltpu.VMEM((side, 8, width), jnp.bfloat16),
            pltpu.VMEM((side, 8, width), jnp.bfloat16),
            pltpu.SMEM(neighbours.shape, jnp.int32),
            pltpu.SMEM(orients.shape, jnp.int32),
            pltpu.SMEM((count,), jnp.int32),
            pltpu.SemaphoreType.DMA((6,)),
        ],
        compiler_params=params(60),
        name="pack_borders",
    )(me, neighbours, orients, out_grad[0])
    packed = after(me, slots)
    if even:
        shard = after(weight, slots).reshape(1, -1, LANES)
        shard = jnp.pad(shard, ((0, 0), (0, -shard.shape[1] % 16), (0, 0)))
        held = jnp.concatenate([shard, from_offset(shard, count, 1)], axis=0)
    slots = lax.all_to_all(slots, "tile", 0, 0, tiled=True)

    inner, edges = pl.pallas_call(
        functools.partial(inner_term, side, width),
        out_shape=(
            jax.ShapeDtypeStruct(sums, jnp.float32),
            jax.ShapeDtypeStruct((width, 4 * side), jnp.bfloat16),
        ),
        in_specs=[SMEM, VMEM, VMEM],
        out_specs=(VMEM, VMEM),
        scratch_shapes=[pltpu.VMEM((width, pixels), jnp.bfloat16)] + shifted,
        compiler_params=params(20),
        cost_estimate=pl.CostEstimate(
            flops=18 * pixels * width * width, bytes_accessed=6 << 20, transcendentals=0
        ),
        name="inner_term",
    )(packed, flat_in, grad)

    if even:
        keep, send = pl.pallas_call(
            functools.partial(rim_term, side, width, chips, pairs),
            out_shape=(
                jax.ShapeDtypeStruct((chips,) + message, jnp.float32),
                jax.ShapeDtypeStruct((chips,) + message, jnp.int16),
            ),
            in_specs=[SMEM, SMEM, VMEM, VMEM, VMEM],
            out_specs=(VMEM,) * 2,
            scratch_shapes=[
                pltpu.VMEM(sums, jnp.float32),
                pltpu.VMEM((2,) + message, jnp.float32),
            ],
            compiler_params=params(20),
            name="rim_term",
        )(after(me, held), neighbours, edges, slots, inner)
        second = from_offset(held, count, 2)
        third = from_offset(held, count, 4)
        own, got, crossing = spread_sums(count, pairs, message, me, keep, send)
        third = after(third, crossing, second)
        last = after(from_offset(third, count, 2), own, got[2])
        held = jnp.concatenate([held, second, third, last], axis=0)
        other = lax.ppermute(after(held, own), "tile", [(i, i ^ 1) for i in range(count)])
        input_grad = pl.pallas_call(
            functools.partial(input_term, side, width, pairs, chips),
            out_shape=jax.ShapeDtypeStruct((pixels, width), jnp.bfloat16),
            in_specs=[SMEM, SMEM] + [VMEM] * 4,
            out_specs=VMEM,
            scratch_shapes=[
                pltpu.VMEM((3 * width, 3 * lanes), jnp.bfloat16),
                pltpu.VMEM((2, 5 * pairs, LANES), jnp.float32),
                pltpu.VMEM(sums, jnp.float32),
            ]
            + shifted,
            compiler_params=params(26),
            cost_estimate=pl.CostEstimate(
                flops=18 * pixels * width * width, bytes_accessed=6 << 20, transcendentals=0
            ),
            name="input_term",
        )(me, neighbours, grad, slots, held, other)
        weight_grad = pl.pallas_call(
            functools.partial(final_sum, pairs, scale),
            out_shape=jax.ShapeDtypeStruct((5 * pairs, LANES), jnp.float32),
            in_specs=[VMEM] * (count // 4),
            out_specs=VMEM,
            compiler_params=params(8),
            name="final_sum",
        )(after(own, input_grad), *got).reshape(-1)
    else:
        parts = pl.pallas_call(
            functools.partial(add_rim, side, width),
            out_shape=jax.ShapeDtypeStruct(sums, jnp.float32),
            in_specs=[SMEM, SMEM, VMEM, VMEM, VMEM],
            out_specs=VMEM,
            compiler_params=params(20),
            name="add_rim",
        )(me, neighbours, edges, slots, inner)
        flat_sums = jnp.concatenate(list(parts), axis=1)[:, :width].reshape(-1)
        weight_grad = scale * lax.psum_scatter(
            flat_sums, "tile", scatter_dimension=0, tiled=True
        )
        input_grad = pl.pallas_call(
            functools.partial(plain_input_term, side, width),
            out_shape=jax.ShapeDtypeStruct((pixels, width), jnp.bfloat16),
            in_specs=[SMEM, SMEM] + [VMEM] * 3,
            out_specs=VMEM,
            scratch_shapes=[pltpu.VMEM((3 * width, 3 * lanes), jnp.bfloat16)] + shifted,
            compiler_params=params(26),
            name="plain_input_term",
        )(me, neighbours, grad, slots, flat_kernel)
    return (input_grad.reshape(inputs.shape), weight_grad)


def spread_sums(count, pairs, message, me, keep, send):
    rows = count // 4
    several = jax.ShapeDtypeStruct((rows,) + message, jnp.float32)
    coded_several = jax.ShapeDtypeStruct((rows,) + message, jnp.int16)
    got = lax.ppermute(send, "tile", [(i, i ^ 1) for i in range(count)])
    keep, send = pl.pallas_call(
        functools.partial(pair_sum, pairs, count // 2),
        out_shape=(several, coded_several),
        in_specs=[SMEM, VMEM, VMEM],
        out_specs=(VMEM,) * 2,
        compiler_params=params(12),
        name="pair_sum",
    )(me, keep, got)
    crossing = send
    got = from_offset(send, count, 1)
    own, *sends = pl.pallas_call(
        functools.partial(cross_sum, pairs, rows),
        out_shape=(jax.ShapeDtypeStruct(message, jnp.float32),)
        + (jax.ShapeDtypeStruct(message, jnp.int16),) * (rows - 1),
        in_specs=[SMEM, VMEM, VMEM],
        out_specs=(VMEM,) * rows,
        compiler_params=params(12),
        name="cross_sum",
    )(me, keep, got)
    got = [from_offset(sends[offset - 1], count, 2 * offset) for offset in range(1, rows)]
    return own, got, crossing


def solution(mesh):
    in_specs = (
        P(("rep", "tile"), None, None, None),
        P(("rep", "tile"), None, None, None),
        P("tile"),
        P(),
        P(),
    )
    out_specs = (P(("rep", "tile"), None, None, None), P(("rep", "tile")))
    return jax.shard_map(
        per_device, mesh=mesh, in_specs=in_specs, out_specs=out_specs, check_vma=False
    )
```

```python
import functools
import math

import jax
import jax.numpy as jnp
from jax import lax
from jax.experimental import pallas as pl
from jax.experimental.pallas import tpu as pltpu
from jax.sharding import PartitionSpec as P

LANES = 128
GROUP = 96
VMEM = pl.BlockSpec(memory_space=pltpu.VMEM)
SMEM = pl.BlockSpec(memory_space=pltpu.SMEM)
HBM = pl.BlockSpec(memory_space=pltpu.HBM)
STRIP_OF = (
    (2, 4, 1, 7),
    (0, 6, 3, 5),
    (6, 3, 5, 0),
    (4, 1, 7, 2),
    (3, 2, 0, 1),
    (2, 0, 1, 3),
    (1, 3, 2, 0),
    (0, 1, 3, 2),
)


def strip_code(direction):
    return sum(strip << (4 * turn) for turn, strip in enumerate(STRIP_OF[direction]))


def params(megabytes):
    return pltpu.CompilerParams(vmem_limit_bytes=megabytes << 20)


def low_half(rows):
    return lax.broadcasted_iota(jnp.int32, (rows, LANES), 1) < LANES // 2


def pick_pixels(rows, target, pixels, flat):
    column = lax.broadcasted_iota(jnp.int32, (rows, pixels), 1)
    pick = jnp.where(column == target, 1.0, 0.0).astype(jnp.bfloat16)
    return jnp.dot(pick, flat, preferred_element_type=jnp.float32)


def edge_pixels(side):
    row = lax.broadcasted_iota(jnp.int32, (4 * side, 1), 0)
    edge, along = row // side, row % side
    return jnp.where(
        edge == 0,
        along,
        jnp.where(
            edge == 1,
            (side - 1) * side + along,
            jnp.where(edge == 2, along * side, along * side + side - 1),
        ),
    )


def widened(block, width):
    return jnp.concatenate(
        [block, jnp.zeros((block.shape[0], 3 * LANES - width), block.dtype)], axis=1
    )


def pack_borders(
    side, count,
    me_ref, nbr_in_ref, turn_in_ref, grad_in_ref,
    slots_ref,
    strips_ref, top_ref, bottom_ref, left_ref, right_ref, nbr_ref, turn_ref, which_ref, sems,
):
    near = left_ref.shape[1]
    half = side // 2
    copies = [
        pltpu.make_async_copy(source, held, sems.at[place])
        for place, (source, held) in enumerate(
            (
                (grad_in_ref.at[:, pl.ds(0, near)], left_ref),
                (grad_in_ref.at[:, pl.ds(side - near, near)], right_ref),
                (grad_in_ref.at[0], top_ref),
                (grad_in_ref.at[side - 1], bottom_ref),
                (nbr_in_ref, nbr_ref),
                (turn_in_ref, turn_ref),
            )
        )
    ]
    for copy in copies:
        copy.start()
    row = lax.broadcasted_iota(jnp.int32, (8 * side, 1), 0)
    edge = row // side % 4
    along = jnp.where(row < 4 * side, row % side, side - 1 - row % side)
    target = jnp.where(
        edge < 2,
        edge * side + along,
        2 * side + jnp.where(edge == 2, along * near, (side + along) * near + near - 1),
    )
    known = 2 * side + 2 * side * near
    column = lax.broadcasted_iota(jnp.int32, (8 * side, known), 1)
    pick = jnp.where(column == target, 1.0, 0.0).astype(jnp.bfloat16)
    low = low_half(half)
    me = me_ref[0]
    for copy in copies[4:]:
        copy.wait()

    def choose(dest, carry):
        which = jnp.int32(0)
        for direction in range(8):
            turn = turn_ref[direction, dest]
            found = (strip_code(direction) >> (4 * turn)) & 15
            which = jnp.where(nbr_ref[direction, dest] == me, found, which)
        which_ref[dest] = which
        return carry

    lax.fori_loop(0, count, choose, 0, unroll=4)
    for copy in copies[:4]:
        copy.wait()
    width = top_ref.shape[1]
    pixels = jnp.concatenate(
        [
            top_ref[...],
            bottom_ref[...],
            left_ref[...].reshape(side * near, width),
            right_ref[...].reshape(side * near, width),
        ],
        axis=0,
    )
    found = widened(jnp.dot(pick, pixels, preferred_element_type=jnp.float32), width)
    for strip in range(8):
        block = found[strip * side : (strip + 1) * side]
        last = block[:, 2 * LANES :]
        last = jnp.where(low, last[:half], pltpu.roll(last[half:], LANES // 2, 1))
        strips_ref[strip % 4 * 2 + strip // 4] = jnp.concatenate(
            [block[:, :LANES], block[:, LANES : 2 * LANES], last], axis=0
        ).astype(jnp.bfloat16)

    def fill(dest, carry):
        slots_ref[dest] = strips_ref[which_ref[dest]]
        return carry

    lax.fori_loop(0, count, fill, 0, unroll=8)


def rim_pieces(side, me_ref, nbr_ref, slots_ref):
    half = side // 2
    low = low_half(side)
    rims = []
    for direction in range(8):
        slot = slots_ref[nbr_ref[direction, me_ref[0]]].astype(jnp.float32)
        last = slot[2 * side :]
        last = jnp.concatenate([last, pltpu.roll(last, LANES // 2, 1)], axis=0)
        last = jnp.where(low, last, 0.0)
        rims.append(jnp.concatenate([slot[:side], slot[side : 2 * side], last], axis=1))
    return rims


def row_shifts(side, rim, first, last):
    place = lax.broadcasted_iota(jnp.int32, rim.shape, 0)
    after = jnp.where(place == side - 1, last, pltpu.roll(rim, side - 1, 0))
    before = jnp.where(place == 0, first, pltpu.roll(rim, 1, 0))
    return (after, rim, before)


def fill_shifted(side, own, rims, ref):
    pixels, lanes = own.shape
    tall = (side, side, lanes)
    place = lax.broadcasted_iota(jnp.int32, tall, 1)
    after = pltpu.roll(own, pixels - 1, 0).reshape(tall)
    before = pltpu.roll(own, 1, 0).reshape(tall)
    if rims is None:
        after = jnp.where(place == side - 1, 0.0, after)
        before = jnp.where(place == 0, 0.0, before)
        outer = [[jnp.zeros((side, lanes), jnp.float32)] * 3] * 2
    else:
        north, south, west, east, nw, ne, sw, se = rims
        after = jnp.where(place == side - 1, east.reshape(side, 1, lanes), after)
        before = jnp.where(place == 0, west.reshape(side, 1, lanes), before)
        outer = [
            row_shifts(side, north, nw[0:1], ne[0:1]),
            row_shifts(side, south, sw[0:1], se[0:1]),
        ]
    for tap, block in enumerate((after.reshape(own.shape), own, before.reshape(own.shape))):
        place = slice(tap * lanes, (tap + 1) * lanes)
        ref[0:side, place] = outer[0][tap].astype(jnp.bfloat16)
        ref[side : side + pixels, place] = block.astype(jnp.bfloat16)
        ref[side + pixels :, place] = outer[1][tap].astype(jnp.bfloat16)


def exponent_of(peak):
    return jnp.maximum(jnp.ceil(jnp.log2(jnp.maximum(peak, 1e-30))), -90.0)


def coded(block):
    power = exponent_of(jnp.max(jnp.abs(block), axis=0, keepdims=True))
    steps = jnp.round(block * (jnp.exp2(15.0 - power) * 0.999)).astype(jnp.int32)
    return steps, power.astype(jnp.int32)


def write_coded(out_ref, block, rows):
    steps, power = coded(block)
    row = lax.broadcasted_iota(jnp.int32, block.shape, 0)
    out_ref[...] = jnp.where(row == rows, power, steps).astype(jnp.int16)


def read_coded(steps, rows):
    whole = steps.astype(jnp.int32)
    power = whole[rows : rows + 1].astype(jnp.float32)
    row = lax.broadcasted_iota(jnp.int32, whole.shape, 0)
    value = whole.astype(jnp.float32) * (jnp.exp2(power - 15.0) * (1.0 / 0.999))
    return jnp.where(row == rows, 0.0, value)


def inner_term(side, width, packed_ref, in_ref, grad_ref, acc_ref, edge_ref, in_t_ref, shifted):
    pixels = side * side
    own = widened(grad_ref[...].astype(jnp.float32), width)
    fill_shifted(side, own, None, shifted)
    edges = pick_pixels(4 * side, edge_pixels(side), pixels, in_ref[...])
    edge_ref[...] = edges.T.astype(jnp.bfloat16)
    in_t_ref[...] = in_ref[...].T
    for row_tap in range(3):
        window = shifted[(2 - row_tap) * side : (2 - row_tap) * side + pixels]
        term = jnp.dot(in_t_ref[...], window, preferred_element_type=jnp.float32)
        for col_tap in range(3):
            tap = 3 * row_tap + col_tap
            for part in range(3):
                place = (3 * col_tap + part) * LANES
                acc_ref[part, tap * width : (tap + 1) * width] = term[:, place : place + LANES]


def add_rim(side, width, me_ref, nbr_ref, edge_ref, slots_ref, inner_ref, acc_ref):
    north, south, west, east, nw, ne, sw, se = rim_pieces(side, me_ref, nbr_ref, slots_ref)
    none = jnp.zeros_like(north)
    tops = row_shifts(side, north, nw[0:1], ne[0:1])
    bottoms = row_shifts(side, south, sw[0:1], se[0:1])
    lefts = row_shifts(side, west, 0.0, 0.0)
    rights = row_shifts(side, east, 0.0, 0.0)
    for row_tap in range(3):
        for col_tap in range(3):
            tap = 3 * row_tap + col_tap
            rows = slice(tap * width, (tap + 1) * width)
            if tap == 4:
                for part in range(3):
                    acc_ref[part, rows] = inner_ref[part, rows]
                continue
            outside = jnp.concatenate(
                [
                    tops[col_tap] if row_tap == 2 else none,
                    bottoms[col_tap] if row_tap == 0 else none,
                    lefts[row_tap] if col_tap == 2 else none,
                    rights[row_tap] if col_tap == 0 else none,
                ],
                axis=0,
            ).astype(jnp.bfloat16)
            term = jnp.dot(edge_ref[...], outside, preferred_element_type=jnp.float32)
            for part in range(3):
                acc_ref[part, rows] = (
                    inner_ref[part, rows] + term[:, part * LANES : (part + 1) * LANES]
                )


def rim_term(
    side, width, chips, pairs,
    me_ref, nbr_ref, edge_ref, slots_ref, inner_ref,
    keep_ref, send_ref,
    acc_ref, pack_ref,
):
    add_rim(side, width, me_ref, nbr_ref, edge_ref, slots_ref, inner_ref, acc_ref)
    half = LANES // 2
    low = low_half(pairs)
    core = me_ref[0] % 2
    blank = jnp.zeros((GROUP - pairs, LANES), jnp.float32)
    for chip in range(chips):
        for shard, out_ref in (
            (2 * chip + core, keep_ref.at[chip]),
            (2 * chip + 1 - core, pack_ref.at[chip % 2]),
        ):
            base = shard * 2 * pairs
            even = pl.ds(base, pairs, stride=2)
            odd = pl.ds(base + 1, pairs, stride=2)
            e0, e1, e2 = [acc_ref[part, even] for part in range(3)]
            o0, o1, o2 = [pltpu.roll(acc_ref[part, odd], half, 1) for part in range(3)]
            groups = (
                e0,
                e1,
                jnp.where(low, e2, o0),
                jnp.where(low, o0, o1),
                jnp.where(low, o1, o2),
            )
            for group, block in enumerate(groups):
                out_ref[group * GROUP : group * GROUP + pairs] = block
                out_ref[group * GROUP + pairs : (group + 1) * GROUP] = blank
        write_coded(send_ref.at[chip], pack_ref[chip % 2], pairs)


def pair_sum(pairs, chips, me_ref, keep_ref, got_ref, own_ref, send_ref):
    across = me_ref[0] // 2 % 2
    for row in range(chips // 2):
        mine = 2 * row + across
        own_ref[row] = keep_ref[mine] + read_coded(got_ref[mine], pairs)
        theirs = 2 * row + 1 - across
        write_coded(
            send_ref.at[row], keep_ref[theirs] + read_coded(got_ref[theirs], pairs), pairs
        )


def cross_sum(pairs, rows, me_ref, keep_ref, got_ref, own_ref, *send_refs):
    for offset in range(rows):
        row = (me_ref[0] // 4) ^ offset
        total = keep_ref[row] + read_coded(got_ref[row], pairs)
        if offset == 0:
            own_ref[...] = total
        else:
            write_coded(send_refs[offset - 1], total, pairs)


def final_sum(pairs, scale, own_ref, *refs):
    got_refs, out_ref, rows_ref = refs[:-2], refs[-2], refs[-1]
    total = own_ref[...]
    for got_ref in got_refs:
        total = total + read_coded(got_ref[...], pairs)
    total = total * scale
    for group in range(5):
        rows_ref[pl.ds(group, GROUP, stride=5), :] = total[group * GROUP : (group + 1) * GROUP]
    out_ref[...] = rows_ref[: out_ref.shape[0]]


def unpack_kernel(pairs, chips, me_ref, mine_ref, other_ref, shard_ref, rows_ref):
    chip = me_ref[0] // 2
    core = me_ref[0] % 2
    half = LANES // 2
    low = low_half(pairs)
    turn = 0
    for offset in range(chips):
        for source_ref, from_core in ((mine_ref, core), (other_ref, 1 - core)):
            shard = 2 * (chip ^ offset) + from_core
            base = shard * 2 * pairs
            even = pl.ds(base, pairs, stride=2)
            odd = pl.ds(base + 1, pairs, stride=2)
            shard_ref[turn, : source_ref.shape[1]] = source_ref[offset].astype(jnp.float32)
            parts = [shard_ref[turn, pl.ds(group, pairs, stride=5), :] for group in range(5)]
            turned = [pltpu.roll(part, half, 1) for part in parts[2:]]
            rows_ref[0, even] = parts[0]
            rows_ref[1, even] = parts[1]
            rows_ref[2, even] = parts[2]
            rows_ref[0, odd] = jnp.where(low, turned[0], turned[1])
            rows_ref[1, odd] = jnp.where(low, turned[1], turned[2])
            rows_ref[2, odd] = turned[2]
            turn = 1 - turn


def input_sums(side, width, me_ref, nbr_ref, grad_ref, slots_ref, kernel_ref, out_ref, shifted):
    own = widened(grad_ref[...].astype(jnp.float32), width)
    fill_shifted(side, own, rim_pieces(side, me_ref, nbr_ref, slots_ref), shifted)
    pixels = side * side
    main = 2 * LANES
    rest = width - main
    total = jnp.zeros((pixels, main), jnp.float32)
    for row_tap in range(3):
        total = total + lax.dot_general(
            shifted[(2 - row_tap) * side : (2 - row_tap) * side + pixels],
            kernel_ref[row_tap * width : row_tap * width + main],
            (((1,), (1,)), ((), ())),
            preferred_element_type=jnp.float32,
        )
    out_ref[:, :main] = total.astype(jnp.bfloat16)
    tails = lax.dot_general(
        shifted[...],
        jnp.concatenate(
            [kernel_ref[tap * width + main : (tap + 1) * width] for tap in range(3)], axis=0
        ),
        (((1,), (1,)), ((), ())),
        preferred_element_type=jnp.float32,
    )
    first = tails[2 * side : 2 * side + pixels, :rest]
    second = tails[side : side + pixels, rest : 2 * rest]
    third = tails[:pixels, 2 * rest :]
    out_ref[:, main:] = (first + second + third).astype(jnp.bfloat16)


def plain_input_term(
    side, width, me_ref, nbr_ref, grad_ref, slots_ref, flat_ref, out_ref, kernel_ref, shifted
):
    for tap in range(9):
        rows = widened(flat_ref[tap * width : (tap + 1) * width].astype(jnp.float32), width)
        place = tap % 3 * rows.shape[1]
        kernel_ref[
            tap // 3 * width : (tap // 3 + 1) * width, place : place + rows.shape[1]
        ] = rows.astype(jnp.bfloat16)
    input_sums(side, width, me_ref, nbr_ref, grad_ref, slots_ref, kernel_ref, out_ref, shifted)


def input_term(
    side, width, pairs, chips,
    me_ref, nbr_ref, grad_ref, slots_ref, mine_ref, other_ref,
    out_ref,
    kernel_ref, shard_ref, rows_ref, shifted,
):
    unpack_kernel(pairs, chips, me_ref, mine_ref, other_ref, shard_ref, rows_ref)
    for tap in range(9):
        for part in range(3):
            place = (tap % 3 * 3 + part) * LANES
            kernel_ref[
                tap // 3 * width : (tap // 3 + 1) * width, place : place + LANES
            ] = rows_ref[part, tap * width : (tap + 1) * width].astype(jnp.bfloat16)
    input_sums(side, width, me_ref, nbr_ref, grad_ref, slots_ref, kernel_ref, out_ref, shifted)


def after(value, *others):
    return lax.optimization_barrier((value,) + others)[0]


def from_offset(value, count, offset):
    return lax.ppermute(value, "tile", [(i, i ^ (2 * offset)) for i in range(count)])


def per_device(inputs, out_grad, weight, neighbours, orients):
    side, width = inputs.shape[1], inputs.shape[3]
    pixels = side * side
    count = lax.axis_size("tile")
    chips = count // 2
    whole = 9 * width * width
    lanes = 3 * LANES
    me = lax.axis_index("tile").reshape(1)
    neighbours, orients = neighbours.T, orients.T
    grad = out_grad.reshape(pixels, width)
    flat_in = inputs.reshape(pixels, width)
    scale = 1.0 / math.sqrt(count * inputs.shape[0] * pixels)
    slot = (5 * side // 2, LANES)
    shifted = [pltpu.VMEM((pixels + 2 * side, 3 * lanes), jnp.bfloat16)]
    sums = (3, 9 * width, LANES)
    padded_sums = (3, 9 * width + 16, LANES)
    even = count == 16 and whole % (2 * width * count) == 0
    pairs = whole // (2 * width * count)
    message = (5 * GROUP, LANES)

    if not even:
        flat_kernel = lax.all_gather(weight, "tile", axis=0, tiled=True).reshape(9 * width, width)

    slots = pl.pallas_call(
        functools.partial(pack_borders, side, count),
        out_shape=jax.ShapeDtypeStruct((count,) + slot, jnp.bfloat16),
        in_specs=[SMEM, HBM, HBM, HBM],
        out_specs=VMEM,
        scratch_shapes=[
            pltpu.VMEM((8,) + slot, jnp.bfloat16),
            pltpu.VMEM((side, width), jnp.bfloat16),
            pltpu.VMEM((side, width), jnp.bfloat16),
            pltpu.VMEM((side, 8, width), jnp.bfloat16),
            pltpu.VMEM((side, 8, width), jnp.bfloat16),
            pltpu.SMEM(neighbours.shape, jnp.int32),
            pltpu.SMEM(orients.shape, jnp.int32),
            pltpu.SMEM((count,), jnp.int32),
            pltpu.SemaphoreType.DMA((6,)),
        ],
        compiler_params=params(60),
        name="pack_borders",
    )(me, neighbours, orients, out_grad[0])
    packed = after(me, slots)
    if even:
        shard = after(weight, slots).reshape(1, -1, LANES)
        shard = jnp.pad(shard, ((0, 0), (0, -shard.shape[1] % 16), (0, 0)))
        held = jnp.concatenate([shard, from_offset(shard, count, 1)], axis=0)
    slots = lax.all_to_all(slots, "tile", 0, 0, tiled=True)

    inner, edges = pl.pallas_call(
        functools.partial(inner_term, side, width),
        out_shape=(
            jax.ShapeDtypeStruct(sums, jnp.float32),
            jax.ShapeDtypeStruct((width, 4 * side), jnp.bfloat16),
        ),
        in_specs=[SMEM, VMEM, VMEM],
        out_specs=(VMEM, VMEM),
        scratch_shapes=[pltpu.VMEM((width, pixels), jnp.bfloat16)] + shifted,
        compiler_params=params(20),
        cost_estimate=pl.CostEstimate(
            flops=18 * pixels * width * width, bytes_accessed=6 << 20, transcendentals=0
        ),
        name="inner_term",
    )(packed, flat_in, grad)

    if even:
        keep, send = pl.pallas_call(
            functools.partial(rim_term, side, width, chips, pairs),
            out_shape=(
                jax.ShapeDtypeStruct((chips,) + message, jnp.float32),
                jax.ShapeDtypeStruct((chips,) + message, jnp.int16),
            ),
            in_specs=[SMEM, SMEM, VMEM, VMEM, VMEM],
            out_specs=(VMEM,) * 2,
            scratch_shapes=[
                pltpu.VMEM(padded_sums, jnp.float32),
                pltpu.VMEM((2,) + message, jnp.float32),
            ],
            compiler_params=params(20),
            name="rim_term",
        )(after(me, held), neighbours, edges, slots, inner)
        second = from_offset(held, count, 2)
        third = from_offset(held, count, 4)
        own, got, crossing = spread_sums(count, pairs, message, me, keep, send)
        third = after(third, crossing, second)
        last = after(from_offset(third, count, 2), own, got[2])
        held = jnp.concatenate([held, second, third, last], axis=0)
        other = lax.ppermute(after(held, own), "tile", [(i, i ^ 1) for i in range(count)])
        input_grad = pl.pallas_call(
            functools.partial(input_term, side, width, pairs, chips),
            out_shape=jax.ShapeDtypeStruct((pixels, width), jnp.bfloat16),
            in_specs=[SMEM, SMEM] + [VMEM] * 4,
            out_specs=VMEM,
            scratch_shapes=[
                pltpu.VMEM((3 * width, 3 * lanes), jnp.bfloat16),
                pltpu.VMEM((2, 5 * GROUP, LANES), jnp.float32),
                pltpu.VMEM(padded_sums, jnp.float32),
            ]
            + shifted,
            compiler_params=params(26),
            cost_estimate=pl.CostEstimate(
                flops=18 * pixels * width * width, bytes_accessed=6 << 20, transcendentals=0
            ),
            name="input_term",
        )(me, neighbours, grad, slots, held, other)
        weight_grad = pl.pallas_call(
            functools.partial(final_sum, pairs, scale),
            out_shape=jax.ShapeDtypeStruct((5 * pairs, LANES), jnp.float32),
            in_specs=[VMEM] * (count // 4),
            out_specs=VMEM,
            scratch_shapes=[pltpu.VMEM(message, jnp.float32)],
            compiler_params=params(8),
            name="final_sum",
        )(after(own, input_grad), *got).reshape(-1)
    else:
        parts = pl.pallas_call(
            functools.partial(add_rim, side, width),
            out_shape=jax.ShapeDtypeStruct(sums, jnp.float32),
            in_specs=[SMEM, SMEM, VMEM, VMEM, VMEM],
            out_specs=VMEM,
            compiler_params=params(20),
            name="add_rim",
        )(me, neighbours, edges, slots, inner)
        flat_sums = jnp.concatenate(list(parts), axis=1)[:, :width].reshape(-1)
        weight_grad = scale * lax.psum_scatter(
            flat_sums, "tile", scatter_dimension=0, tiled=True
        )
        input_grad = pl.pallas_call(
            functools.partial(plain_input_term, side, width),
            out_shape=jax.ShapeDtypeStruct((pixels, width), jnp.bfloat16),
            in_specs=[SMEM, SMEM] + [VMEM] * 3,
            out_specs=VMEM,
            scratch_shapes=[pltpu.VMEM((3 * width, 3 * lanes), jnp.bfloat16)] + shifted,
            compiler_params=params(26),
            name="plain_input_term",
        )(me, neighbours, grad, slots, flat_kernel)
    return (input_grad.reshape(inputs.shape), weight_grad)


def spread_sums(count, pairs, message, me, keep, send):
    rows = count // 4
    several = jax.ShapeDtypeStruct((rows,) + message, jnp.float32)
    coded_several = jax.ShapeDtypeStruct((rows,) + message, jnp.int16)
    got = lax.ppermute(send, "tile", [(i, i ^ 1) for i in range(count)])
    keep, send = pl.pallas_call(
        functools.partial(pair_sum, pairs, count // 2),
        out_shape=(several, coded_several),
        in_specs=[SMEM, VMEM, VMEM],
        out_specs=(VMEM,) * 2,
        compiler_params=params(12),
        name="pair_sum",
    )(me, keep, got)
    crossing = send
    got = from_offset(send, count, 1)
    own, *sends = pl.pallas_call(
        functools.partial(cross_sum, pairs, rows),
        out_shape=(jax.ShapeDtypeStruct(message, jnp.float32),)
        + (jax.ShapeDtypeStruct(message, jnp.int16),) * (rows - 1),
        in_specs=[SMEM, VMEM, VMEM],
        out_specs=(VMEM,) * rows,
        compiler_params=params(12),
        name="cross_sum",
    )(me, keep, got)
    got = [from_offset(sends[offset - 1], count, 2 * offset) for offset in range(1, rows)]
    return own, got, crossing


def solution(mesh):
    in_specs = (
        P(("rep", "tile"), None, None, None),
        P(("rep", "tile"), None, None, None),
        P("tile"),
        P(),
        P(),
    )
    out_specs = (P(("rep", "tile"), None, None, None), P(("rep", "tile")))
    return jax.shard_map(
        per_device, mesh=mesh, in_specs=in_specs, out_specs=out_specs, check_vma=False
    )
```
